128 devices in a mesh: gx: 16 (over x, z), gy: 8 (over y, core).
Axes of the slice: x: 4, y: 4, z: 4, core: 2. Of those that a mesh axis runs over, the one named last changes fastest.
Arguments:
- particles: float32 [4, 262144], P(None, ('gx', 'gy')), may hold values from -1 to 1, as said below
- tree_cells: float32 [10, 1048576], P(None, ('gx', 'gy')), may hold values from -1 to 1, as said below
- let_list: int32 [128, 128, 4], P(('gx', 'gy')), may hold values from 0 to 63
- let_count: int32 [128, 128], P(('gx', 'gy')), may hold values from 1 to 4, as said below
- part_list: int32 [128, 4, 4], P(('gx', 'gy')), may hold values from 0 to 15
- cell_lists: int32 [2048, 16], P(('gx', 'gy')), may hold values from 0 to 575
- near_lists: int32 [2048, 8], P(('gx', 'gy')), may hold values from 0 to 31
Outputs:
- forces: float32 [4, 262144], P(None, ('gx', 'gy'))
The draws below stay inside these ranges and needn't reach their ends.
Inputs may be any that keep to these rules, and one draw needn't show every extreme that they name: let_count is 4 wherever sender and receiver are at most 2 apart along gx+gy, and between 1 and 4 elsewhere. `particles`: positions lie in [-1, 1], masses are positive. `tree_cells`: centres lie in [-1, 1], masses are positive, the quadrupole is traceless.
All inputs are finite; a program needn't handle non-finite values.
Results may differ from the reference program's by a relative error of at most 0.0003.
Values sent between devices are 32-bit elements; how exact they have to be, the bound alone decides.
A program may use at most 64 MiB of HBM per device.

```python
import math
import jax
import jax.numpy as jnp
from jax import lax

NBLK = 16
NCB = 64
BLK = 128
SLOTS = 4
BPB = 4
LC = 16
LP = 8
DEVICES = 128


def draw_particles(key, part):
    keys = jax.random.split(key, 2)
    count = NBLK * BLK * DEVICES
    centre = jax.random.uniform(keys[0], (3, count), jnp.float32, -1.0, 1.0)
    masses = jnp.exp(jax.random.uniform(keys[1], (1, count), jnp.float32, math.log(0.0001), math.log(0.001)))
    return jnp.concatenate([centre, masses], axis=0)


def draw_tree_cells(key, part):
    keys = jax.random.split(key, 3)
    count = NCB * BLK * DEVICES
    centre = jax.random.uniform(keys[0], (3, count), jnp.float32, -1.0, 1.0)
    masses = jnp.exp(jax.random.uniform(keys[1], (1, count), jnp.float32, math.log(0.0005), math.log(0.005)))
    shape_terms = jax.random.normal(keys[2], (5, count), jnp.float32) * 0.08 * masses
    quad_xx = shape_terms[0:1]
    quad_yy = shape_terms[1:2]
    quad_zz = -(quad_xx + quad_yy)
    return jnp.concatenate([centre, masses, quad_xx, quad_yy, quad_zz, shape_terms[2:5]], axis=0)


def draw_let_count(key, part):
    senders = jnp.arange(DEVICES, dtype=jnp.int32)[:, None]
    receivers = jnp.arange(DEVICES, dtype=jnp.int32)[None, :]
    nearby = jnp.abs(senders - receivers) <= 2
    farther = jax.random.randint(key, (DEVICES, DEVICES), 1, SLOTS + 1, dtype=jnp.int32)
    return jnp.where(nearby, jnp.int32(SLOTS), farther).astype(jnp.int32)


def set_ends(values, stream_key, least, high):
    longest = values.shape.index(max(values.shape))
    spots = []
    for shift in (0, 1):
        where = [jax.random.randint(jax.random.fold_in(stream_key, axis), (), 0, length) for axis, length in enumerate(values.shape)]
        where[longest] = (where[longest] + shift) % values.shape[longest]
        spots.append(tuple(where))
    return values.at[spots[0]].set(least).at[spots[1]].set(high)


def setup_inputs(seed: int = 0) -> dict:
    streams_of = jax.random.split(jax.random.key(seed), 8)
    particles = draw_particles(jax.random.fold_in(streams_of[7], 71), 0)
    tree_cells = draw_tree_cells(jax.random.fold_in(streams_of[7], 71), 0)
    let_list = set_ends(jax.random.randint(streams_of[2], (DEVICES, DEVICES, SLOTS), 0, NCB), jax.random.fold_in(streams_of[2], 1), 0, NCB - 1).astype(jnp.int32)
    let_count = draw_let_count(jax.random.fold_in(streams_of[7], 71), 0)
    part_list = set_ends(jax.random.randint(streams_of[4], (DEVICES, 4, BPB), 0, NBLK), jax.random.fold_in(streams_of[4], 1), 0, NBLK - 1).astype(jnp.int32)
    cell_lists = set_ends(jax.random.randint(streams_of[5], (DEVICES * NBLK, LC), 0, NCB + DEVICES * SLOTS), jax.random.fold_in(streams_of[5], 1), 0, (NCB + DEVICES * SLOTS) - 1).astype(jnp.int32)
    near_lists = set_ends(jax.random.randint(streams_of[6], (DEVICES * NBLK, LP), 0, NBLK + 4 * BPB), jax.random.fold_in(streams_of[6], 1), 0, (NBLK + 4 * BPB) - 1).astype(jnp.int32)
    return {"particles": particles, "tree_cells": tree_cells, "let_list": let_list, "let_count": let_count, "part_list": part_list, "cell_lists": cell_lists, "near_lists": near_lists}


SOFTENING = 0.0025
near_offsets = (1, -1, 2, -2)

def pair_forces(targets, cell_source, near_source):
    target_x = targets[0][:, None]
    target_y = targets[1][:, None]
    target_z = targets[2][:, None]
    delta_x = target_x - cell_source[0][None, :]
    delta_y = target_y - cell_source[1][None, :]
    delta_z = target_z - cell_source[2][None, :]
    inverse = 1.0 / jnp.sqrt(delta_x * delta_x + delta_y * delta_y + delta_z * delta_z + SOFTENING)
    inv_square = inverse * inverse
    inv_cube = inverse * inv_square
    inv_five = inv_cube * inv_square
    masses = cell_source[3][None, :]
    quad_x = cell_source[4][None, :] * delta_x + cell_source[7][None, :] * delta_y + cell_source[8][None, :] * delta_z
    quad_y = cell_source[7][None, :] * delta_x + cell_source[5][None, :] * delta_y + cell_source[9][None, :] * delta_z
    quad_z = cell_source[8][None, :] * delta_x + cell_source[9][None, :] * delta_y + cell_source[6][None, :] * delta_z
    contracted = delta_x * quad_x + delta_y * quad_y + delta_z * quad_z
    radial = -masses * inv_cube - 2.5 * contracted * inv_five * inv_square
    accel_x = lax.optimization_barrier(jnp.sum(radial * delta_x + quad_x * inv_five, axis=1))
    accel_y = lax.optimization_barrier(jnp.sum(radial * delta_y + quad_y * inv_five, axis=1))
    accel_z = lax.optimization_barrier(jnp.sum(radial * delta_z + quad_z * inv_five, axis=1))
    potential = lax.optimization_barrier(jnp.sum(-masses * inverse - 0.5 * contracted * inv_five, axis=1))
    near_x = target_x - near_source[0][None, :]
    near_y = target_y - near_source[1][None, :]
    near_z = target_z - near_source[2][None, :]
    near_inverse = 1.0 / jnp.sqrt(near_x * near_x + near_y * near_y + near_z * near_z + SOFTENING)
    near_masses = near_source[3][None, :]
    near_radial = -near_masses * near_inverse * near_inverse * near_inverse
    accel_x = accel_x + lax.optimization_barrier(jnp.sum(near_radial * near_x, axis=1))
    accel_y = accel_y + lax.optimization_barrier(jnp.sum(near_radial * near_y, axis=1))
    accel_z = accel_z + lax.optimization_barrier(jnp.sum(near_radial * near_z, axis=1))
    potential = potential + lax.optimization_barrier(jnp.sum(-near_masses * near_inverse, axis=1))
    return jnp.stack([accel_x, accel_y, accel_z, potential])

def block_forces(own_parts, cell_pool, near_pool, cell_ids, near_ids):

    def one_block(carried):
        targets, cell_row, near_row = carried
        cell_source = cell_pool[:, cell_row].reshape(10, -1)
        near_source = near_pool[:, near_row].reshape(4, -1)
        return pair_forces(targets, cell_source, near_source)
    result = lax.map(one_block, (jnp.moveaxis(own_parts, 1, 0), cell_ids, near_ids))
    return jnp.moveaxis(result, 0, 1).reshape(4, -1)

def reference(particles, tree_cells, let_list, let_count, part_list, cell_lists, near_lists):
    all_parts = particles.reshape(4, DEVICES, NBLK, BLK)
    all_cells = tree_cells.reshape(10, DEVICES, NCB, BLK)
    source_ids = jnp.arange(DEVICES, dtype=jnp.int32)
    slot_ids = jnp.arange(SLOTS, dtype=jnp.int32)
    cell_rows = cell_lists.reshape(DEVICES, NBLK, LC)
    near_rows = near_lists.reshape(DEVICES, NBLK, LP)

    def one_device(device):
        block_ids = let_list[:, device, :]
        received = all_cells[:, source_ids[:, None], block_ids]
        live_mask = slot_ids[None, :] < let_count[:, device][:, None]
        received = jnp.where(live_mask[None, :, :, None], received, jnp.float32(0.0))
        own_cells = all_cells[:, device]
        cell_pool = jnp.concatenate([own_cells, received.reshape(10, DEVICES * SLOTS, BLK)], axis=1)
        own_parts = all_parts[:, device]
        near_parts = [own_parts]
        for position, offset in enumerate(near_offsets):
            source = device - offset
            source_valid = (source >= 0) & (source < DEVICES)
            source_safe = jnp.clip(source, 0, DEVICES - 1).astype(jnp.int32)
            picked = all_parts[:, source_safe][:, part_list[source_safe, position]]
            near_parts.append(jnp.where(source_valid, picked, jnp.float32(0.0)))
        near_pool = jnp.concatenate(near_parts, axis=1)
        return block_forces(own_parts, cell_pool, near_pool, cell_rows[device], near_rows[device])
    result = lax.map(one_device, source_ids)
    return jnp.moveaxis(result, 0, 1).reshape(4, -1)
```

```python
import jax
import jax.numpy as jnp
from jax import lax
from jax.experimental import pallas as pl
from jax.experimental.pallas import tpu as pltpu
from jax.sharding import PartitionSpec as P

BLK = 128
NBLK = 16
NCB = 64
DEV = 128
LC = 16
LP = 8
ROWS = 9
EPS = 0.0025
MESH = pl.DeviceIdType.MESH
near_offsets = (1, -1, 2, -2)

ZERO = NCB + 2 * DEV
APOOL = ZERO + 1
NA = 9

f32 = jnp.float32
i32 = jnp.int32


def rows_of(ref, block, count):
    return [jnp.broadcast_to(ref[block, r], (8, BLK)) for r in range(count)]


def cell_item(t_ref, t_base, pool, block, acc):
    X, Y, Z, M, Qxx, Qyy, Qxy, Qxz, Qyz = rows_of(pool, block, ROWS)
    Qzz = -(Qxx + Qyy)

    def tile(t, carry):
        s = pl.ds(pl.multiple_of(t * 8, 8), 8)
        x = t_ref[t_base, s] - X
        y = t_ref[t_base + 1, s] - Y
        z = t_ref[t_base + 2, s] - Z
        u = lax.rsqrt(x * x + y * y + z * z + EPS)
        u2 = u * u
        qx = Qxx * x + Qxy * y + Qxz * z
        qy = Qxy * x + Qyy * y + Qyz * z
        qz = Qxz * x + Qyz * y + Qzz * z
        v = (x * qx + y * qy + z * qz) * (u2 * u2)
        u3 = u * u2
        p = u3 * (M + 2.5 * v)
        u5 = u3 * u2
        acc[0, s] += p * x - u5 * qx
        acc[1, s] += p * y - u5 * qy
        acc[2, s] += p * z - u5 * qz
        acc[3, s] += u * (M + 0.5 * v)
        return carry

    lax.fori_loop(0, 16, tile, 0, unroll=True)


def near_item(t_ref, t_base, pool, block, acc):
    X, Y, Z, M = rows_of(pool, block, 4)

    def tile(t, carry):
        s = pl.ds(pl.multiple_of(t * 8, 8), 8)
        x = t_ref[t_base, s] - X
        y = t_ref[t_base + 1, s] - Y
        z = t_ref[t_base + 2, s] - Z
        u = lax.rsqrt(x * x + y * y + z * z + EPS)
        mu = M * u
        p = mu * (u * u)
        acc[0, s] += p * x
        acc[1, s] += p * y
        acc[2, s] += p * z
        acc[3, s] += mu
        return carry

    lax.fori_loop(0, 16, tile, 0, unroll=True)


def lane_totals(acc):
    lane = lax.broadcasted_iota(i32, (BLK, BLK), 1)
    packed = jnp.zeros((BLK, BLK), f32)
    for k in range(4):
        total = jnp.sum(acc[k], axis=1, keepdims=True)
        packed = jnp.where(lane == k, jnp.broadcast_to(total, (BLK, BLK)), packed)
    return -jnp.transpose(packed)[:8]


def spread_targets(parts, t_ref, j, base):
    cols = jnp.transpose(parts[:, pl.ds(pl.multiple_of(j * BLK, BLK), BLK)])
    for c in range(3):
        t_ref[base + c] = jnp.broadcast_to(cols[:, c : c + 1], (BLK, BLK))


def exchange_kernel(
    let_list, let_count, part_list, near_lists, cell_lists, parts, cells,
    part_out, a_out, b_out,
    own_cells, own_rows, chosen_a, chosen_b, apool, npick, npool, t_ref, acc, list_v, list_s,
    send_a, recv_a, send_b, recv_b, send_n, recv_n, local_sem,
):
    gx = lax.axis_index("gx")
    gy = lax.axis_index("gy")
    me = gx * 8 + gy
    cx, cz = gx // 4, lax.rem(gx, 4)
    cy, cc = gy // 2, lax.rem(gy, 2)

    barrier = pltpu.get_barrier_semaphore()

    def greet(i, carry):
        d = lax.rem(me + i, DEV)
        pl.semaphore_signal(
            barrier, inc=1, device_id=(d // 8, lax.rem(d, 8)), device_id_type=MESH
        )
        return carry

    lax.fori_loop(1, DEV, greet, 0)

    order = (0, 1, 2, 3, 4, 5, 7, 8, 9)

    def own_block(b, carry):
        at = pl.ds(pl.multiple_of(b * BLK, BLK), BLK)
        for r, source in enumerate(order):
            row = cells[source : source + 1, at]
            own_cells[b, r] = row
            apool[b, r] = row
        return carry

    lax.fori_loop(0, NCB, own_block, 0)
    for r in range(ROWS):
        apool[ZERO, r] = jnp.zeros((1, BLK), f32)

    def own_parts(b, carry):
        at = pl.ds(pl.multiple_of(b * BLK, BLK), BLK)
        for r in range(4):
            row = parts[r : r + 1, at]
            own_rows[b, r] = row
            npool[b, r] = row
        return carry

    lax.fori_loop(0, NBLK, own_parts, 0)

    for position, offset in enumerate(near_offsets):
        target = me + offset
        keep = jnp.where((target >= 0) & (target < DEV), 1.0, 0.0).astype(f32)
        for b in range(4):
            pick = own_rows[part_list[position * 4 + b]]
            npick[position * 4 + b] = pick * keep

    def choose(d, carry):
        count = let_count[d]
        for k in range(4):
            live = jnp.where(k < count, 1.0, 0.0).astype(f32)
            block = own_cells[let_list[d * 4 + k]] * live
            if k < 2:
                chosen_a[d * 2 + k] = block
            else:
                chosen_b[d * 2 + k - 2] = block
        return carry

    lax.fori_loop(0, DEV, choose, 0)

    ids = cell_lists[...]
    lane = lax.broadcasted_iota(i32, (NBLK, BLK), 1)
    remote = ids - NCB
    slot = remote & 3
    early = ((ids < NCB) | (slot < 2)) & (lane < LC)
    place = jnp.where(ids < NCB, ids, NCB + 2 * (remote >> 2) + slot)
    rank = early.astype(i32)
    for shift in (1, 2, 4, 8):
        rank = rank + jnp.where(lane >= shift, pltpu.roll(rank, shift, 1), 0)
    packed = jnp.full((NBLK, BLK), ZERO, i32)
    for p in range(NA):
        hit = jnp.where(early & (rank == p + 1), ZERO - place, 0)
        found = jnp.sum(hit, axis=1, keepdims=True)
        packed = jnp.where(lane == p, ZERO - found, packed)
    list_v[...] = packed
    to_smem = pltpu.make_async_copy(list_v, list_s, local_sem)
    to_smem.start()
    to_smem.wait()

    def spread(j, carry):
        spread_targets(parts, t_ref, j, j * 3)
        return carry

    lax.fori_loop(0, NBLK, spread, 0)

    pl.semaphore_wait(barrier, DEV - 1)

    for position, offset in enumerate(near_offsets):
        d = lax.rem(me + offset + DEV, DEV)
        pltpu.make_async_remote_copy(
            npick.at[pl.ds(position * 4, 4)],
            npool.at[pl.ds(NBLK + position * 4, 4)],
            send_n.at[position],
            recv_n.at[position],
            device_id=(d // 8, lax.rem(d, 8)),
            device_id_type=MESH,
        ).start()

    def send_pairs(chosen, pool, base, send, recv):
        def send_one(i, carry):
            dx = lax.rem(i, 4)
            dy = lax.rem(i // 4 + dx, 4)
            dz = lax.rem(i // 16 + 2 * dx + dy, 4)
            ngx = lax.rem(cx + dx, 4) * 4 + lax.rem(cz + dz, 4)
            ngy = lax.rem(cy + dy, 4) * 2 + lax.rem(cc + i // 64, 2)
            d = ngx * 8 + ngy
            pltpu.make_async_remote_copy(
                chosen.at[pl.ds(d * 2, 2)],
                pool.at[pl.ds(base + me * 2, 2)],
                send,
                recv,
                device_id=(ngx, ngy),
                device_id_type=MESH,
            ).start()
            return carry

        lax.fori_loop(1, DEV, send_one, 0)

    def pair_wait(chosen, pool, base, send, recv):
        pltpu.make_async_remote_copy(
            chosen.at[pl.ds(0, 2 * DEV - 2)],
            pool.at[pl.ds(base, 2 * DEV - 2)],
            send,
            recv,
            device_id=(gx, gy),
            device_id_type=MESH,
        ).wait()

    send_pairs(chosen_a, apool, NCB, send_a, recv_a)
    send_pairs(chosen_b, b_out, 0, send_b, recv_b)
    own_a = pltpu.make_async_copy(
        chosen_a.at[pl.ds(me * 2, 2)], apool.at[pl.ds(NCB + me * 2, 2)], local_sem
    )
    own_a.start()
    own_a.wait()
    own_b = pltpu.make_async_copy(
        chosen_b.at[pl.ds(me * 2, 2)], b_out.at[pl.ds(me * 2, 2)], local_sem
    )
    own_b.start()
    own_b.wait()

    for position in range(4):
        pltpu.make_async_remote_copy(
            npick.at[pl.ds(position * 4, 4)],
            npool.at[pl.ds(NBLK + position * 4, 4)],
            send_n.at[position],
            recv_n.at[position],
            device_id=(gx, gy),
            device_id_type=MESH,
        ).wait()

    def near_block(j, carry):
        acc[j] = jnp.zeros((4, BLK, BLK), f32)

        def item(i, inner):
            near_item(t_ref, j * 3, npool, near_lists[j * LP + i], acc.at[j])
            return inner

        lax.fori_loop(0, LP, item, 0)
        return carry

    lax.fori_loop(0, NBLK, near_block, 0)

    pair_wait(chosen_a, apool, NCB, send_a, recv_a)
    keep_a = pltpu.make_async_copy(apool, a_out, local_sem)
    keep_a.start()

    def cell_block(j, carry):
        def item(i, inner):
            cell_item(t_ref, j * 3, apool, list_s[j, i], acc.at[j])
            return inner

        lax.fori_loop(0, NA, item, 0)
        part_out[j] = lane_totals(acc.at[j])
        return carry

    lax.fori_loop(0, NBLK, cell_block, 0)

    keep_a.wait()
    pair_wait(chosen_b, b_out, 0, send_b, recv_b)


def rest_kernel(
    cell_lists, parts, partial, a_in, b_in, out,
    pool, t_ref, acc, live_v, live_s, items, sem,
):
    copy_a = pltpu.make_async_copy(a_in, pool.at[pl.ds(0, APOOL)], sem.at[0])
    copy_b = pltpu.make_async_copy(b_in, pool.at[pl.ds(APOOL, 2 * DEV)], sem.at[1])
    copy_a.start()
    copy_b.start()
    copy_b.wait()
    masses = pool[pl.ds(APOOL, 2 * DEV), 3].reshape(2 * DEV, BLK)
    for h in range(2):
        flipped = jnp.transpose(masses[h * DEV : (h + 1) * DEV])
        live_v[h : h + 1] = (flipped[:1] > 0).astype(i32)
    to_smem = pltpu.make_async_copy(live_v, live_s, sem.at[1])
    to_smem.start()
    to_smem.wait()
    copy_a.wait()

    def block(j, carry):
        acc[...] = jnp.zeros((4, BLK, BLK), f32)
        spread_targets(parts, t_ref, j, 0)

        def pick(i, state):
            rank, n = state
            c = cell_lists[j * LC + i]
            own = c < NCB
            remote = jnp.where(own, 0, c - NCB)
            slot = remote & 3
            sender = remote >> 2
            early = own | (slot < 2)
            late = jnp.where(early, 0, sender * 2 + slot - 2)
            live = live_s[late >> 7, late & 127]
            rank = rank + early.astype(i32)
            todo = jnp.where(early, (rank > NA).astype(i32), live)
            place = jnp.where(own, c, NCB + 2 * sender + slot)
            items[n] = jnp.where(early, place, APOOL + late)
            return rank, n + todo

        rank, n = lax.fori_loop(0, LC, pick, (jnp.int32(0), jnp.int32(0)))

        def item(i, inner):
            cell_item(t_ref, 0, pool, items[i], acc)
            return inner

        lax.fori_loop(0, n, item, 0)
        total = lane_totals(acc) + partial[j]
        out[:, pl.ds(pl.multiple_of(j * BLK, BLK), BLK)] = total[:4]
        return carry

    lax.fori_loop(0, NBLK, block, 0)


def body(particles, tree_cells, let_list, let_count, part_list, cell_lists, near_lists):
    smem = pl.BlockSpec(memory_space=pltpu.SMEM)
    vmem = pl.BlockSpec(memory_space=pltpu.VMEM)
    hbm = pl.BlockSpec(memory_space=pl.ANY)
    block = (ROWS, 1, BLK)
    padded = jnp.pad(cell_lists, ((0, 0), (0, BLK - LC)))
    partial, a_pool, b_pool = pl.pallas_call(
        exchange_kernel,
        out_shape=(
            jax.ShapeDtypeStruct((NBLK, 8, BLK), f32),
            jax.ShapeDtypeStruct((APOOL, *block), f32),
            jax.ShapeDtypeStruct((2 * DEV, *block), f32),
        ),
        in_specs=[smem] * 4 + [vmem] * 3,
        out_specs=(vmem, hbm, hbm),
        scratch_shapes=[
            pltpu.VMEM((NCB, *block), f32),
            pltpu.VMEM((NBLK, 4, 1, BLK), f32),
            pltpu.VMEM((2 * DEV, *block), f32),
            pltpu.VMEM((2 * DEV, *block), f32),
            pltpu.VMEM((APOOL, *block), f32),
            pltpu.VMEM((16, 4, 1, BLK), f32),
            pltpu.VMEM((2 * NBLK, 4, 1, BLK), f32),
            pltpu.VMEM((3 * NBLK, BLK, BLK), f32),
            pltpu.VMEM((NBLK, 4, BLK, BLK), f32),
            pltpu.VMEM((NBLK, BLK), i32),
            pltpu.SMEM((NBLK, BLK), i32),
            pltpu.SemaphoreType.DMA,
            pltpu.SemaphoreType.DMA,
            pltpu.SemaphoreType.DMA,
            pltpu.SemaphoreType.DMA,
            pltpu.SemaphoreType.DMA((4,)),
            pltpu.SemaphoreType.DMA((4,)),
            pltpu.SemaphoreType.DMA,
        ],
        compiler_params=pltpu.CompilerParams(
            collective_id=0, has_side_effects=True, vmem_limit_bytes=60 << 20
        ),
        name="exchange",
    )(
        let_list.reshape(-1), let_count.reshape(-1), part_list.reshape(-1),
        near_lists.reshape(-1), padded, particles, tree_cells,
    )
    return pl.pallas_call(
        rest_kernel,
        out_shape=jax.ShapeDtypeStruct(particles.shape, f32),
        in_specs=[smem, vmem, vmem, hbm, hbm],
        out_specs=vmem,
        scratch_shapes=[
            pltpu.VMEM((APOOL + 2 * DEV, *block), f32),
            pltpu.VMEM((3, BLK, BLK), f32),
            pltpu.VMEM((4, BLK, BLK), f32),
            pltpu.VMEM((8, BLK), i32),
            pltpu.SMEM((8, BLK), i32),
            pltpu.SMEM((LC + 1,), i32),
            pltpu.SemaphoreType.DMA((2,)),
        ],
        compiler_params=pltpu.CompilerParams(vmem_limit_bytes=60 << 20),
        name="rest",
    )(cell_lists.reshape(-1), particles, partial, a_pool, b_pool)


def solution(mesh):
    return jax.shard_map(
        body,
        mesh=mesh,
        in_specs=(
            P(None, ("gx", "gy")),
            P(None, ("gx", "gy")),
            P(("gx", "gy"), None, None),
            P(("gx", "gy"), None),
            P(("gx", "gy"), None, None),
            P(("gx", "gy"), None),
            P(("gx", "gy"), None),
        ),
        out_specs=P(None, ("gx", "gy")),
        check_vma=False,
    )
```

```python
import jax
import jax.numpy as jnp
from jax import lax
from jax.experimental import pallas as pl
from jax.experimental.pallas import tpu as pltpu
from jax.sharding import PartitionSpec as P

BLK = 128
NBLK = 16
NCB = 64
DEV = 128
LC = 16
LP = 8
ROWS = 9
EPS = 0.0025
MESH = pl.DeviceIdType.MESH
near_offsets = (1, -1, 2, -2)

OWN = NCB * ROWS
PAIR = 2 * ROWS + 1
ZERO = OWN + DEV * PAIR
AROWS = ZERO + ROWS
LATE = 2 * ROWS
BROWS = DEV * LATE
NA = 9
SPILL = LC - NA

f32 = jnp.float32
i32 = jnp.int32


def rows_of(ref, first, count):
    return [jnp.broadcast_to(ref[first + r], (8, BLK)) for r in range(count)]


def cell_item(t_ref, t_base, pool, first, acc):
    X, Y, Z, M, Qxx, Qyy, Qxy, Qxz, Qyz = rows_of(pool, first, ROWS)
    Qzz = -(Qxx + Qyy)

    def tile(t, carry):
        s = pl.ds(pl.multiple_of(t * 8, 8), 8)
        x = t_ref[t_base, s] - X
        y = t_ref[t_base + 1, s] - Y
        z = t_ref[t_base + 2, s] - Z
        u = lax.rsqrt(x * x + y * y + z * z + EPS)
        u2 = u * u
        qx = Qxx * x + Qxy * y + Qxz * z
        qy = Qxy * x + Qyy * y + Qyz * z
        qz = Qxz * x + Qyz * y + Qzz * z
        v = (x * qx + y * qy + z * qz) * (u2 * u2)
        u3 = u * u2
        p = u3 * (M + 2.5 * v)
        u5 = u3 * u2
        acc[0, s] += p * x - u5 * qx
        acc[1, s] += p * y - u5 * qy
        acc[2, s] += p * z - u5 * qz
        acc[3, s] += u * (M + 0.5 * v)
        return carry

    lax.fori_loop(0, 16, tile, 0, unroll=True)


def near_item(t_ref, t_base, pool, block, acc):
    X, Y, Z, M = rows_of(pool, block * 4, 4)

    def tile(t, carry):
        s = pl.ds(pl.multiple_of(t * 8, 8), 8)
        x = t_ref[t_base, s] - X
        y = t_ref[t_base + 1, s] - Y
        z = t_ref[t_base + 2, s] - Z
        u = lax.rsqrt(x * x + y * y + z * z + EPS)
        mu = M * u
        p = mu * (u * u)
        acc[0, s] += p * x
        acc[1, s] += p * y
        acc[2, s] += p * z
        acc[3, s] += mu
        return carry

    lax.fori_loop(0, 16, tile, 0, unroll=True)


def lane_totals(acc):
    lane = lax.broadcasted_iota(i32, (BLK, BLK), 1)
    packed = jnp.zeros((BLK, BLK), f32)
    for k in range(4):
        total = jnp.sum(acc[k], axis=1, keepdims=True)
        packed = jnp.where(lane == k, jnp.broadcast_to(total, (BLK, BLK)), packed)
    return -jnp.transpose(packed)[:8]


def exchange_kernel(
    let_in, count_in, part_in, near_in, cell_in, parts_in, cells_in,
    acc, t_ref, apool, bpool, late_lists,
    let_list, let_count, part_list, near_lists, cell_lists, cells, parts, own_cells, own_rows, chosen_a, chosen_b, npick, npool,
    ids_v, count_v, list_v, list_s,
    send_a, recv_a, send_b, recv_b, send_n, recv_n, local_sem,
):
    gx = lax.axis_index("gx")
    gy = lax.axis_index("gy")
    me = gx * 8 + gy
    cx, cz = gx // 4, lax.rem(gx, 4)
    cy, cc = gy // 2, lax.rem(gy, 2)

    barrier = pltpu.get_barrier_semaphore()

    def greet(i, carry):
        d = lax.rem(me + i, DEV)
        pl.semaphore_signal(
            barrier, inc=1, device_id=(d // 8, lax.rem(d, 8)), device_id_type=MESH
        )
        return carry

    loads = [
        pltpu.make_async_copy(source, target, local_sem.at[n])
        for n, (source, target) in enumerate(
            (
                (cells_in, cells),
                (parts_in, parts),
                (let_in, let_list),
                (count_in, let_count),
                (part_in, part_list),
                (near_in, near_lists),
                (cell_in, cell_lists),
            )
        )
    ]
    for load in loads:
        load.start()
    lax.fori_loop(1, DEV, greet, 0, unroll=8)
    for load in loads:
        load.wait()

    order = (0, 1, 2, 3, 4, 5, 7, 8, 9)

    def own_block(b, carry):
        at = pl.ds(pl.multiple_of(b * BLK, BLK), BLK)
        for r, source in enumerate(order):
            own_cells[b * ROWS + r] = cells[source : source + 1, at]
        return carry

    lax.fori_loop(0, NCB, own_block, 0, unroll=8)

    def own_parts(b, carry):
        at = pl.ds(pl.multiple_of(b * BLK, BLK), BLK)
        for r in range(4):
            own_rows[b * 4 + r] = parts[r : r + 1, at]
        return carry

    lax.fori_loop(0, NBLK, own_parts, 0, unroll=8)

    for position, offset in enumerate(near_offsets):
        target = me + offset
        keep = jnp.where((target >= 0) & (target < DEV), 1.0, 0.0).astype(f32)
        for b in range(4):
            first = part_list[position, b] * 4
            for r in range(4):
                npick[position * 16 + b * 4 + r] = own_rows[first + r] * keep

    def choose(d, carry):
        count = let_count[0, d]
        for k in range(4):
            live = jnp.where(k < count, 1.0, 0.0).astype(f32)
            first = let_list[k, d] * ROWS
            for r in range(ROWS):
                row = own_cells[first + r] * live
                if k < 2:
                    chosen_a[d * PAIR + k * ROWS + r] = row
                else:
                    chosen_b[d * LATE + (k - 2) * ROWS + r] = row
        chosen_a[d * PAIR + 2 * ROWS] = jnp.full((1, BLK), count.astype(f32))
        return carry

    lax.fori_loop(0, DEV, choose, 0, unroll=4)

    for r in range(ROWS):
        apool[ZERO + r] = jnp.zeros((1, BLK), f32)

    pl.semaphore_wait(barrier, DEV - 1)

    for position, offset in enumerate(near_offsets):
        d = lax.rem(me + offset + DEV, DEV)
        pltpu.make_async_remote_copy(
            npick.at[pl.ds(position * 16, 16)],
            npool.at[pl.ds(NBLK * 4 + position * 16, 16)],
            send_n.at[position],
            recv_n.at[position],
            device_id=(d // 8, lax.rem(d, 8)),
            device_id_type=MESH,
        ).start()

    def send_all(chosen, pool, base, rows, send, recv):
        def send_one(i, carry):
            dx = lax.rem(i, 4)
            dy = lax.rem(i // 4 + dx, 4)
            dz = lax.rem(i // 16 + 2 * dx + dy, 4)
            ngx = lax.rem(cx + dx, 4) * 4 + lax.rem(cz + dz, 4)
            ngy = lax.rem(cy + dy, 4) * 2 + lax.rem(cc + i // 64, 2)
            d = ngx * 8 + ngy
            pltpu.make_async_remote_copy(
                chosen.at[pl.ds(d * rows, rows)],
                pool.at[pl.ds(base + me * rows, rows)],
                send,
                recv,
                device_id=(ngx, ngy),
                device_id_type=MESH,
            ).start()
            return carry

        lax.fori_loop(1, DEV, send_one, 0, unroll=2)

    def wait_all(chosen, pool, base, rows, send, recv):
        pltpu.make_async_remote_copy(
            chosen.at[pl.ds(0, (DEV - 1) * rows)],
            pool.at[pl.ds(base, (DEV - 1) * rows)],
            send,
            recv,
            device_id=(gx, gy),
            device_id_type=MESH,
        ).wait()

    send_all(chosen_a, apool, OWN, PAIR, send_a, recv_a)

    own_copies = (
        pltpu.make_async_copy(
            own_cells, apool.at[pl.ds(0, OWN)], local_sem.at[0]
        ),
        pltpu.make_async_copy(
            chosen_a.at[pl.ds(me * PAIR, PAIR)],
            apool.at[pl.ds(OWN + me * PAIR, PAIR)],
            local_sem.at[1],
        ),
        pltpu.make_async_copy(
            chosen_b.at[pl.ds(me * LATE, LATE)],
            bpool.at[pl.ds(me * LATE, LATE)],
            local_sem.at[2],
        ),
        pltpu.make_async_copy(
            own_rows, npool.at[pl.ds(0, NBLK * 4)], local_sem.at[3]
        ),
    )
    for copy in own_copies:
        copy.start()

    def spread(j, carry):
        at = pl.ds(pl.multiple_of(j * BLK, BLK), BLK)
        cols = jnp.transpose(parts[:, at])
        for c in range(3):
            t_ref[j * 3 + c] = jnp.broadcast_to(cols[:, c : c + 1], (BLK, BLK))
        return carry

    lax.fori_loop(0, NBLK, spread, 0, unroll=4)

    for copy in own_copies:
        copy.wait()
    for position in range(4):
        pltpu.make_async_remote_copy(
            npick.at[pl.ds(position * 16, 16)],
            npool.at[pl.ds(NBLK * 4 + position * 16, 16)],
            send_n.at[position],
            recv_n.at[position],
            device_id=(gx, gy),
            device_id_type=MESH,
        ).wait()

    def near_block(j, carry):
        acc[j] = jnp.zeros((4, BLK, BLK), f32)

        def item(i, inner):
            near_item(t_ref, j * 3, npool, near_lists[i, j], acc.at[j])
            return inner

        lax.fori_loop(0, LP, item, 0)
        return carry

    lax.fori_loop(0, 10, near_block, 0)
    send_all(chosen_b, bpool, 0, LATE, send_b, recv_b)
    lax.fori_loop(10, NBLK, near_block, 0)

    wait_all(chosen_a, apool, OWN, PAIR, send_a, recv_a)

    row_lane = lax.broadcasted_iota(i32, (1, BLK), 1)

    def gather_counts(j, carry):
        ids = jnp.full((1, BLK), -1, i32)
        counts = jnp.zeros((1, BLK), f32)
        for i in range(LC):
            c = cell_lists[j, i]
            sender = jnp.maximum(c - NCB, 0) >> 2
            here = row_lane == i
            ids = jnp.where(here, c, ids)
            counts = jnp.where(here, apool[OWN + sender * PAIR + 2 * ROWS], counts)
        ids_v[j] = ids
        count_v[j] = counts
        return carry

    lax.fori_loop(0, NBLK, gather_counts, 0, unroll=2)
    ids = ids_v[...].reshape(NBLK, BLK)
    counts = count_v[...].reshape(NBLK, BLK)
    lane = lax.broadcasted_iota(i32, (NBLK, BLK), 1)
    remote = jnp.maximum(ids - NCB, 0)
    slot = remote & 3
    sender = remote >> 2
    own = ids < NCB
    live = (ids >= 0) & (own | (slot.astype(f32) < counts))
    early = live & (own | (slot < 2))
    late = live & (ids >= NCB) & (slot >= 2)
    early_row = jnp.where(own, ids * ROWS, OWN + sender * PAIR + slot * ROWS)
    late_row = sender * LATE + (slot - 2) * ROWS

    def ranks(flags):
        rank = flags.astype(i32)
        for shift in (1, 2, 4, 8):
            rank = rank + jnp.where(lane >= shift, pltpu.roll(rank, shift, 1), 0)
        return rank

    def nth(flags, rank, n, values):
        return jnp.sum(jnp.where(flags & (rank == n), values, 0), axis=1, keepdims=True)

    early_rank = ranks(early)
    late_rank = ranks(late)
    packed = jnp.full((NBLK, BLK), ZERO, i32)
    for p in range(NA):
        gap = nth(early, early_rank, p + 1, ZERO - early_row)
        packed = jnp.where(lane == p, ZERO - gap, packed)
    list_v[...] = packed
    to_smem = pltpu.make_async_copy(list_v, list_s, local_sem.at[0])
    to_smem.start()
    n_early = jnp.sum(early.astype(i32), axis=1, keepdims=True)
    n_late = jnp.sum(late.astype(i32), axis=1, keepdims=True)
    packed = jnp.where(lane == 2 * LC, jnp.maximum(n_early - NA, 0), n_late)
    for p in range(SPILL):
        packed = jnp.where(lane == p, nth(early, early_rank, NA + p + 1, early_row), packed)
    for p in range(LC):
        packed = jnp.where(lane == LC + p, nth(late, late_rank, p + 1, late_row), packed)
    late_lists[...] = packed
    to_smem.wait()

    def cell_block(j, carry):
        def item(i, inner):
            cell_item(t_ref, j * 3, apool, list_s[j, i], acc.at[j])
            return inner

        lax.fori_loop(0, NA, item, 0)
        return carry

    lax.fori_loop(0, NBLK, cell_block, 0)

    wait_all(chosen_b, bpool, 0, LATE, send_b, recv_b)


def rest_kernel(lists, acc_in, t_ref, apool, bpool, out, acc):
    def block(j, carry):
        acc[j] = acc_in[j]

        def spilled(i, inner):
            cell_item(t_ref, j * 3, apool, lists[j, i], acc.at[j])
            return inner

        def item(i, inner):
            cell_item(t_ref, j * 3, bpool, lists[j, LC + i], acc.at[j])
            return inner

        lax.fori_loop(0, lists[j, 2 * LC], spilled, 0)
        lax.fori_loop(0, lists[j, 2 * LC + 1], item, 0)
        return carry

    lax.fori_loop(0, NBLK, block, 0)

    def finish(j, carry):
        out[:, pl.ds(pl.multiple_of(j * BLK, BLK), BLK)] = lane_totals(acc.at[j])[:4]
        return carry

    lax.fori_loop(0, NBLK, finish, 0, unroll=4)


def body(particles, tree_cells, let_list, let_count, part_list, cell_lists, near_lists):
    smem = pl.BlockSpec(memory_space=pltpu.SMEM)
    vmem = pl.BlockSpec(memory_space=pltpu.VMEM)
    hbm = pl.BlockSpec(memory_space=pltpu.HBM)

    def rows(count):
        return pltpu.VMEM((count, 1, BLK), f32)

    acc_shape = (NBLK, 4, BLK, BLK)
    outs = pl.pallas_call(
        exchange_kernel,
        out_shape=(
            pltpu.VMEM(acc_shape, f32),
            pltpu.VMEM((3 * NBLK, BLK, BLK), f32),
            pltpu.VMEM((AROWS, 1, BLK), f32),
            pltpu.VMEM((BROWS, 1, BLK), f32),
            pltpu.VMEM((NBLK, BLK), i32),
        ),
        in_specs=[hbm] * 7,
        out_specs=(vmem,) * 5,
        scratch_shapes=[
            pltpu.SMEM((4, DEV), i32),
            pltpu.SMEM((1, DEV), i32),
            pltpu.SMEM((4, 4), i32),
            pltpu.SMEM((LP, NBLK), i32),
            pltpu.SMEM((NBLK, LC), i32),
            pltpu.VMEM(tree_cells.shape, f32),
            pltpu.VMEM(particles.shape, f32),
            rows(OWN),
            rows(NBLK * 4),
            rows(DEV * PAIR),
            rows(DEV * LATE),
            rows(4 * 16),
            rows(2 * NBLK * 4),
            pltpu.VMEM((NBLK, 1, BLK), i32),
            pltpu.VMEM((NBLK, 1, BLK), f32),
            pltpu.VMEM((NBLK, BLK), i32),
            pltpu.SMEM((NBLK, BLK), i32),
            pltpu.SemaphoreType.DMA,
            pltpu.SemaphoreType.DMA,
            pltpu.SemaphoreType.DMA,
            pltpu.SemaphoreType.DMA,
            pltpu.SemaphoreType.DMA((4,)),
            pltpu.SemaphoreType.DMA((4,)),
            pltpu.SemaphoreType.DMA((7,)),
        ],
        compiler_params=pltpu.CompilerParams(
            collective_id=0, has_side_effects=True, vmem_limit_bytes=24 << 20
        ),
        name="exchange",
    )(
        *[pltpu.with_memory_space_constraint(q, pltpu.HBM) for q in (jnp.transpose(let_list[0]), let_count, part_list[0],
        jnp.transpose(near_lists), cell_lists)], pltpu.with_memory_space_constraint(particles, pltpu.HBM), pltpu.with_memory_space_constraint(tree_cells, pltpu.HBM),
    )
    return pl.pallas_call(
        rest_kernel,
        out_shape=jax.ShapeDtypeStruct(particles.shape, f32),
        in_specs=[smem] + [vmem] * 4,
        out_specs=vmem,
        scratch_shapes=[pltpu.VMEM(acc_shape, f32)],
        compiler_params=pltpu.CompilerParams(vmem_limit_bytes=24 << 20),
        name="rest",
    )(outs[4], *outs[:4])


def solution(mesh):
    return jax.shard_map(
        body,
        mesh=mesh,
        in_specs=(
            P(None, ("gx", "gy")),
            P(None, ("gx", "gy")),
            P(("gx", "gy"), None, None),
            P(("gx", "gy"), None),
            P(("gx", "gy"), None, None),
            P(("gx", "gy"), None),
            P(("gx", "gy"), None),
        ),
        out_specs=P(None, ("gx", "gy")),
        check_vma=False,
    )
```

```python
import jax
import jax.numpy as jnp
from jax import lax
from jax.experimental import pallas as pl
from jax.experimental.pallas import tpu as pltpu
from jax.sharding import PartitionSpec as P

BLK = 128
NBLK = 16
NCB = 64
DEV = 128
LC = 16
LP = 8
ROWS = 9
EPS = 0.0025
MESH = pl.DeviceIdType.MESH
near_offsets = (1, -1, 2, -2)

OWN = NCB * ROWS
ZERO = OWN + DEV * ROWS
ROWS0 = ZERO + ROWS
ONE = ROWS + 1
ROWS1 = DEV * ONE
LATE = 2 * ROWS
ROWS2 = DEV * LATE
N0 = 5
N1 = 3
NEAR_FIRST = 12

f32 = jnp.float32
i32 = jnp.int32


def rows_of(ref, first, count):
    return [jnp.broadcast_to(ref[first + r], (8, BLK)) for r in range(count)]


def rows_of_two(pool0, pool1, entry):
    other = entry >= ROWS0
    first0 = jnp.where(other, 0, entry)
    first1 = jnp.where(other, entry - ROWS0, 0)
    return [
        jnp.broadcast_to(jnp.where(other, pool1[first1 + r], pool0[first0 + r]), (8, BLK))
        for r in range(ROWS)
    ]


def cell_item(t_ref, t_base, rows, acc):
    X, Y, Z, M, Qxx, Qyy, Qxy, Qxz, Qyz = rows
    Qzz = -(Qxx + Qyy)

    def tile(t, carry):
        s = pl.ds(pl.multiple_of(t * 8, 8), 8)
        x = t_ref[t_base, s] - X
        y = t_ref[t_base + 1, s] - Y
        z = t_ref[t_base + 2, s] - Z
        u = lax.rsqrt(x * x + y * y + z * z + EPS)
        u2 = u * u
        qx = Qxx * x + Qxy * y + Qxz * z
        qy = Qxy * x + Qyy * y + Qyz * z
        qz = Qxz * x + Qyz * y + Qzz * z
        v = (x * qx + y * qy + z * qz) * (u2 * u2)
        u3 = u * u2
        p = u3 * (M + 2.5 * v)
        u5 = u3 * u2
        acc[0, s] += p * x - u5 * qx
        acc[1, s] += p * y - u5 * qy
        acc[2, s] += p * z - u5 * qz
        acc[3, s] += u * (M + 0.5 * v)
        return carry

    lax.fori_loop(0, 16, tile, 0, unroll=True)


def near_item(t_ref, t_base, pool, blocks, acc):
    sources = [rows_of(pool, block * 4, 4) for block in blocks]

    def tile(t, carry):
        s = pl.ds(pl.multiple_of(t * 8, 8), 8)
        tx, ty, tz = t_ref[t_base, s], t_ref[t_base + 1, s], t_ref[t_base + 2, s]
        sums = [acc[k, s] for k in range(4)]
        for X, Y, Z, M in sources:
            x = tx - X
            y = ty - Y
            z = tz - Z
            u = lax.rsqrt(x * x + y * y + z * z + EPS)
            mu = M * u
            p = mu * (u * u)
            for k, term in enumerate((p * x, p * y, p * z, mu)):
                sums[k] = sums[k] + term
        for k in range(4):
            acc[k, s] = sums[k]
        return carry

    lax.fori_loop(0, 16, tile, 0, unroll=True)


def lane_totals(acc):
    lane = lax.broadcasted_iota(i32, (BLK, BLK), 1)
    packed = jnp.zeros((BLK, BLK), f32)
    for k in range(4):
        total = jnp.sum(acc[k], axis=1, keepdims=True)
        packed = jnp.where(lane == k, jnp.broadcast_to(total, (BLK, BLK)), packed)
    return -jnp.transpose(packed)[:8]


def ranks(flags, lane):
    rank = flags.astype(i32)
    for shift in (1, 2, 4, 8):
        rank = rank + jnp.where(lane >= shift, pltpu.roll(rank, shift, 1), 0)
    return rank


def nth(flags, rank, n, values):
    return jnp.sum(jnp.where(flags & (rank == n), values, 0), axis=1, keepdims=True)


def exchange_kernel(
    let_in, count_in, part_in, near_in, cell_in, parts_in, cells_in,
    acc, t_ref, pool0, pool1, pool2, left_lists,
    let_list, let_count, part_list, near_lists, cell_lists, cell_ids,
    cells, parts, own_cells, own_rows, chosen0, chosen1, chosen2, npick, npool,
    ids_v, count_v, list_v, list0, list1,
    send_sem, recv_sem, send_n, recv_n, local_sem,
):
    gx = lax.axis_index("gx")
    gy = lax.axis_index("gy")
    me = gx * 8 + gy
    cx, cz = gx // 4, lax.rem(gx, 4)
    cy, cc = gy // 2, lax.rem(gy, 2)
    px = [lax.rem(cx + m, 4) * 4 for m in range(4)]
    py = [lax.rem(cy + m, 4) * 2 for m in range(4)]

    def to_all(action):
        def batch(h, carry, skip=False):
            pz = [lax.rem(cz + h + m, 4) for m in range(4)]
            core = lax.rem(cc + h // 4, 2)
            for b in range(4):
                for a in range(4):
                    if skip and a == 0 and b == 0:
                        continue
                    dy = (a + b) % 4
                    action(px[a] + pz[(2 * a + dy) % 4], py[dy] + core)
            return carry

        batch(0, 0, True)
        lax.fori_loop(1, 8, batch, 0)

    barrier = pltpu.get_barrier_semaphore()

    def greet(ngx, ngy):
        pl.semaphore_signal(barrier, inc=1, device_id=(ngx, ngy), device_id_type=MESH)

    loads = [
        pltpu.make_async_copy(source, target, local_sem.at[n])
        for n, (source, target) in enumerate(
            (
                (cells_in, cells),
                (parts_in, parts),
                (let_in, let_list),
                (count_in, let_count),
                (part_in, part_list),
                (near_in, near_lists),
                (cell_in, cell_lists),
                (cell_in, cell_ids),
            )
        )
    ]
    for load in loads:
        load.start()
    to_all(greet)
    for load in loads:
        load.wait()

    order = (0, 1, 2, 3, 4, 5, 7, 8, 9)

    def own_block(b, carry):
        at = pl.ds(pl.multiple_of(b * BLK, BLK), BLK)
        for r, source in enumerate(order):
            own_cells[b * ROWS + r] = cells[source : source + 1, at]
        return carry

    lax.fori_loop(0, NCB, own_block, 0, unroll=8)

    def own_parts(b, carry):
        at = pl.ds(pl.multiple_of(b * BLK, BLK), BLK)
        for r in range(4):
            own_rows[b * 4 + r] = parts[r : r + 1, at]
        return carry

    lax.fori_loop(0, NBLK, own_parts, 0, unroll=8)

    for position, offset in enumerate(near_offsets):
        target = me + offset
        keep = jnp.where((target >= 0) & (target < DEV), 1.0, 0.0).astype(f32)
        for b in range(4):
            first = part_list[position, b] * 4
            for r in range(4):
                npick[position * 16 + b * 4 + r] = own_rows[first + r] * keep

    def choose0(d, carry):
        first = let_list[0, d] * ROWS
        for r in range(ROWS):
            chosen0[d * ROWS + r] = own_cells[first + r]
        return carry

    lax.fori_loop(0, DEV, choose0, 0, unroll=8)

    pl.semaphore_wait(barrier, DEV - 1)

    for position, offset in enumerate(near_offsets):
        d = lax.rem(me + offset + DEV, DEV)
        pltpu.make_async_remote_copy(
            npick.at[pl.ds(position * 16, 16)],
            npool.at[pl.ds(NBLK * 4 + position * 16, 16)],
            send_n.at[position],
            recv_n.at[position],
            device_id=(d // 8, lax.rem(d, 8)),
            device_id_type=MESH,
        ).start()

    phases = ((chosen0, pool0, OWN, ROWS), (chosen1, pool1, 0, ONE), (chosen2, pool2, 0, LATE))

    def send_all(phase):
        chosen, pool, base, rows = phases[phase]

        def send(ngx, ngy):
            pltpu.make_async_remote_copy(
                chosen.at[pl.ds((ngx * 8 + ngy) * rows, rows)],
                pool.at[pl.ds(base + me * rows, rows)],
                send_sem.at[phase],
                recv_sem.at[phase],
                device_id=(ngx, ngy),
                device_id_type=MESH,
            ).start()

        to_all(send)

    def wait_all(phase):
        chosen, pool, base, rows = phases[phase]
        pltpu.make_async_remote_copy(
            chosen.at[pl.ds(0, (DEV - 1) * rows)],
            pool.at[pl.ds(base, (DEV - 1) * rows)],
            send_sem.at[phase],
            recv_sem.at[phase],
            device_id=(gx, gy),
            device_id_type=MESH,
        ).wait()

    send_all(0)

    def choose_others(d, carry):
        count = let_count[0, d]
        for k, (chosen, base) in enumerate(
            ((chosen1, d * ONE), (chosen2, d * LATE), (chosen2, d * LATE + ROWS)), 1
        ):
            live = jnp.where(k < count, 1.0, 0.0).astype(f32)
            first = let_list[k, d] * ROWS
            for r in range(ROWS):
                chosen[base + r] = own_cells[first + r] * live
        chosen1[d * ONE + ROWS] = jnp.full((1, BLK), count.astype(f32))
        return carry

    lax.fori_loop(0, DEV, choose_others, 0, unroll=4)

    for r in range(ROWS):
        pool0[ZERO + r] = jnp.zeros((1, BLK), f32)

    lane = lax.broadcasted_iota(i32, (NBLK, BLK), 1)
    ids_v[...] = jnp.full((NBLK, BLK), -1, i32)
    ids_v[:, :LC] = cell_ids[...]
    ids = ids_v[...]
    remote = jnp.maximum(ids - NCB, 0)
    slot = remote & 3
    sender = remote >> 2
    listed = ids >= 0
    own = listed & (ids < NCB)
    far = ids >= NCB
    in0 = own | (far & (slot == 0))
    row0 = jnp.where(own, ids * ROWS, OWN + sender * ROWS)
    rank0 = ranks(in0, lane)
    packed = jnp.full((NBLK, BLK), ZERO, i32)
    for p in range(N0):
        packed = jnp.where(lane == p, ZERO - nth(in0, rank0, p + 1, ZERO - row0), packed)
    list_v[...] = packed
    to_list0 = pltpu.make_async_copy(list_v, list0, local_sem.at[7])
    to_list0.start()

    own_copies = [
        pltpu.make_async_copy(own_cells, pool0.at[pl.ds(0, OWN)], local_sem.at[0]),
        pltpu.make_async_copy(own_rows, npool.at[pl.ds(0, NBLK * 4)], local_sem.at[1]),
    ] + [
        pltpu.make_async_copy(
            chosen.at[pl.ds(me * rows, rows)],
            pool.at[pl.ds(base + me * rows, rows)],
            local_sem.at[2 + phase],
        )
        for phase, (chosen, pool, base, rows) in enumerate(phases)
    ]
    for copy in own_copies:
        copy.start()

    send_all(1)

    def spread(j, carry):
        at = pl.ds(pl.multiple_of(j * BLK, BLK), BLK)
        cols = jnp.transpose(parts[:, at])
        for c in range(3):
            t_ref[j * 3 + c] = jnp.broadcast_to(cols[:, c : c + 1], (BLK, BLK))
        return carry

    lax.fori_loop(0, NBLK, spread, 0, unroll=4)

    to_list0.wait()
    for copy in own_copies:
        copy.wait()
    for position in range(4):
        pltpu.make_async_remote_copy(
            npick.at[pl.ds(position * 16, 16)],
            npool.at[pl.ds(NBLK * 4 + position * 16, 16)],
            send_n.at[position],
            recv_n.at[position],
            device_id=(gx, gy),
            device_id_type=MESH,
        ).wait()

    def near_block(j, carry):
        acc[j] = jnp.zeros((4, BLK, BLK), f32)

        def item(i, inner):
            near_item(t_ref, j * 3, npool, [near_lists[i * 2 + k, j] for k in range(2)], acc.at[j])
            return inner

        lax.fori_loop(0, LP // 2, item, 0)
        return carry

    lax.fori_loop(0, NEAR_FIRST, near_block, 0)
    send_all(2)
    lax.fori_loop(NEAR_FIRST, NBLK, near_block, 0)

    wait_all(0)

    def block0(j, carry):
        def item(i, inner):
            cell_item(t_ref, j * 3, rows_of(pool0, list0[j, i], ROWS), acc.at[j])
            return inner

        lax.fori_loop(0, N0, item, 0)
        return carry

    lax.fori_loop(0, NBLK, block0, 0)

    wait_all(1)

    row_lane = lax.broadcasted_iota(i32, (1, BLK), 1)

    def gather_counts(j, carry):
        counts = jnp.zeros((1, BLK), f32)
        for i in range(LC):
            sender_i = jnp.maximum(cell_lists[j, i] - NCB, 0) >> 2
            counts = jnp.where(row_lane == i, pool1[sender_i * ONE + ROWS], counts)
        count_v[j] = counts
        return carry

    lax.fori_loop(0, NBLK, gather_counts, 0, unroll=2)
    counts = count_v[...].reshape(NBLK, BLK)
    live = slot.astype(f32) < counts
    in1 = (in0 & (rank0 > N0)) | (far & (slot == 1) & live)
    in2 = far & (slot >= 2) & live
    row1 = jnp.where(in0, row0, ROWS0 + sender * ONE)
    row2 = sender * LATE + (slot - 2) * ROWS
    rank1 = ranks(in1, lane)
    rank2 = ranks(in2, lane)
    packed = jnp.full((NBLK, BLK), ZERO, i32)
    for p in range(N1):
        packed = jnp.where(lane == p, ZERO - nth(in1, rank1, p + 1, ZERO - row1), packed)
    list_v[...] = packed
    to_list1 = pltpu.make_async_copy(list_v, list1, local_sem.at[0])
    to_list1.start()
    n1 = jnp.sum(in1.astype(i32), axis=1, keepdims=True)
    n2 = jnp.sum(in2.astype(i32), axis=1, keepdims=True)
    packed = jnp.where(lane == 2 * LC, jnp.maximum(n1 - N1, 0), n2)
    for p in range(LC - N1):
        packed = jnp.where(lane == p, nth(in1, rank1, N1 + p + 1, row1), packed)
    for p in range(LC):
        packed = jnp.where(lane == LC + p, nth(in2, rank2, p + 1, row2), packed)
    left_lists[...] = packed
    to_list1.wait()

    def block1(j, carry):
        def item(i, inner):
            cell_item(t_ref, j * 3, rows_of_two(pool0, pool1, list1[j, i]), acc.at[j])
            return inner

        lax.fori_loop(0, N1, item, 0)
        return carry

    lax.fori_loop(0, NBLK, block1, 0)

    wait_all(2)


def rest_kernel(lists, acc_in, t_ref, pool0, pool1, pool2, out, acc):
    def block(j, carry):
        def left(i, inner):
            cell_item(t_ref, j * 3, rows_of_two(pool0, pool1, lists[j, i]), acc.at[j])
            return inner

        def late(i, inner):
            cell_item(t_ref, j * 3, rows_of(pool2, lists[j, LC + i], ROWS), acc.at[j])
            return inner

        lax.fori_loop(0, lists[j, 2 * LC], left, 0)
        lax.fori_loop(0, lists[j, 2 * LC + 1], late, 0)
        return carry

    lax.fori_loop(0, NBLK, block, 0)

    def finish(j, carry):
        out[:, pl.ds(pl.multiple_of(j * BLK, BLK), BLK)] = lane_totals(acc.at[j])[:4]
        return carry

    lax.fori_loop(0, NBLK, finish, 0, unroll=4)


def body(particles, tree_cells, let_list, let_count, part_list, cell_lists, near_lists):
    smem = pl.BlockSpec(memory_space=pltpu.SMEM)
    vmem = pl.BlockSpec(memory_space=pltpu.VMEM)
    hbm = pl.BlockSpec(memory_space=pltpu.HBM)

    def rows(count):
        return pltpu.VMEM((count, 1, BLK), f32)

    acc_shape = (NBLK, 4, BLK, BLK)
    outs = pl.pallas_call(
        exchange_kernel,
        out_shape=(
            pltpu.VMEM(acc_shape, f32),
            pltpu.VMEM((3 * NBLK, BLK, BLK), f32),
            rows(ROWS0),
            rows(ROWS1),
            rows(ROWS2),
            pltpu.VMEM((NBLK, BLK), i32),
        ),
        in_specs=[hbm] * 7,
        out_specs=(vmem,) * 6,
        scratch_shapes=[
            pltpu.SMEM((4, DEV), i32),
            pltpu.SMEM((1, DEV), i32),
            pltpu.SMEM((4, 4), i32),
            pltpu.SMEM((LP, NBLK), i32),
            pltpu.SMEM((NBLK, LC), i32),
            pltpu.VMEM((NBLK, LC), i32),
            pltpu.VMEM(tree_cells.shape, f32),
            pltpu.VMEM(particles.shape, f32),
            rows(OWN),
            rows(NBLK * 4),
            rows(DEV * ROWS),
            rows(DEV * ONE),
            rows(DEV * LATE),
            rows(4 * 16),
            rows(2 * NBLK * 4),
            pltpu.VMEM((NBLK, BLK), i32),
            pltpu.VMEM((NBLK, 1, BLK), f32),
            pltpu.VMEM((NBLK, BLK), i32),
            pltpu.SMEM((NBLK, BLK), i32),
            pltpu.SMEM((NBLK, BLK), i32),
            pltpu.SemaphoreType.DMA((3,)),
            pltpu.SemaphoreType.DMA((3,)),
            pltpu.SemaphoreType.DMA((4,)),
            pltpu.SemaphoreType.DMA((4,)),
            pltpu.SemaphoreType.DMA((8,)),
        ],
        compiler_params=pltpu.CompilerParams(
            collective_id=0, has_side_effects=True, vmem_limit_bytes=24 << 20
        ),
        name="exchange",
    )(
        *[pltpu.with_memory_space_constraint(q, pltpu.HBM) for q in (jnp.transpose(let_list[0]), let_count, part_list[0],
        jnp.transpose(near_lists), cell_lists)], pltpu.with_memory_space_constraint(particles, pltpu.HBM), pltpu.with_memory_space_constraint(tree_cells, pltpu.HBM),
    )
    return pl.pallas_call(
        rest_kernel,
        out_shape=(jax.ShapeDtypeStruct(particles.shape, f32), pltpu.VMEM(acc_shape, f32)),
        in_specs=[smem] + [vmem] * 5,
        out_specs=(vmem, vmem),
        input_output_aliases={1: 1},
        compiler_params=pltpu.CompilerParams(vmem_limit_bytes=24 << 20),
        name="rest",
    )(outs[5], *outs[:5])[0]


def solution(mesh):
    return jax.shard_map(
        body,
        mesh=mesh,
        in_specs=(
            P(None, ("gx", "gy")),
            P(None, ("gx", "gy")),
            P(("gx", "gy"), None, None),
            P(("gx", "gy"), None),
            P(("gx", "gy"), None, None),
            P(("gx", "gy"), None),
            P(("gx", "gy"), None),
        ),
        out_specs=P(None, ("gx", "gy")),
        check_vma=False,
    )
```

```python
import jax
import jax.numpy as jnp
from jax import lax
from jax.experimental import pallas as pl
from jax.experimental.pallas import tpu as pltpu
from jax.sharding import PartitionSpec as P

BLK = 128
NBLK = 16
NCB = 64
DEV = 128
LC = 16
LP = 8
ROWS = 9
EPS = 0.0025
MESH = pl.DeviceIdType.MESH
near_offsets = (1, -1, 2, -2)

OWN = NCB * ROWS
ZERO = OWN + DEV * ROWS
ROWS0 = ZERO + ROWS
ONE = ROWS + 1
ROWS1 = DEV * ONE
LATE = 2 * ROWS
ROWS2 = DEV * LATE
N0 = 4
N1 = 4
NEAR_FIRST = 4

f32 = jnp.float32
i32 = jnp.int32


def rows_of(ref, first, count):
    return [jnp.broadcast_to(ref[first + r], (8, BLK)) for r in range(count)]


def rows_of_two(pool0, pool1, entry):
    other = entry >= ROWS0
    first0 = jnp.where(other, 0, entry)
    first1 = jnp.where(other, entry - ROWS0, 0)
    return [
        jnp.broadcast_to(jnp.where(other, pool1[first1 + r], pool0[first0 + r]), (8, BLK))
        for r in range(ROWS)
    ]


def cell_item(t_ref, t_base, sources, acc):
    def tile(t, carry):
        s = pl.ds(pl.multiple_of(t * 8, 8), 8)
        tx, ty, tz = t_ref[t_base, s], t_ref[t_base + 1, s], t_ref[t_base + 2, s]
        sums = [acc[k, s] for k in range(4)]
        for X, Y, Z, M, Qxx, Qyy, Qxy, Qxz, Qyz in sources:
            x = tx - X
            y = ty - Y
            z = tz - Z
            u = lax.rsqrt(x * x + y * y + z * z + EPS)
            u2 = u * u
            u5 = u * u2 * u2
            x5 = u5 * x
            y5 = u5 * y
            z5 = u5 * z
            qx = Qxx * x5 + Qxy * y5 + Qxz * z5
            qy = Qxy * x5 + Qyy * y5 + Qyz * z5
            qz = Qxz * x5 + Qyz * y5 - (Qxx + Qyy) * z5
            w = x * qx + y * qy + z * qz
            mu = M * u
            p = u2 * (mu + 2.5 * w)
            for k, term in enumerate((p * x - qx, p * y - qy, p * z - qz, mu + 0.5 * w)):
                sums[k] = sums[k] + term
        for k in range(4):
            acc[k, s] = sums[k]
        return carry

    lax.fori_loop(0, 16, tile, 0, unroll=True)


def cell_items(count, rows_at, t_ref, t_base, acc):
    def pair(i, carry):
        cell_item(t_ref, t_base, [rows_at(2 * i), rows_at(2 * i + 1)], acc)
        return carry

    def single(i, carry):
        cell_item(t_ref, t_base, [rows_at(i)], acc)
        return carry

    pairs = count // 2 if isinstance(count, int) else count >> 1
    lax.fori_loop(0, pairs, pair, 0)
    if not isinstance(count, int) or count % 2:
        lax.fori_loop(2 * pairs, count, single, 0)


def near_item(t_ref, t_base, pool, blocks, acc):
    sources = [rows_of(pool, block * 4, 4) for block in blocks]

    def tile(t, carry):
        s = pl.ds(pl.multiple_of(t * 8, 8), 8)
        tx, ty, tz = t_ref[t_base, s], t_ref[t_base + 1, s], t_ref[t_base + 2, s]
        sums = [acc[k, s] for k in range(4)]
        for X, Y, Z, M in sources:
            x = tx - X
            y = ty - Y
            z = tz - Z
            u = lax.rsqrt(x * x + y * y + z * z + EPS)
            mu = M * u
            p = mu * (u * u)
            for k, term in enumerate((p * x, p * y, p * z, mu)):
                sums[k] = sums[k] + term
        for k in range(4):
            acc[k, s] = sums[k]
        return carry

    lax.fori_loop(0, 16, tile, 0, unroll=True)


def lane_totals(acc):
    lane = lax.broadcasted_iota(i32, (BLK, BLK), 1)
    packed = jnp.zeros((BLK, BLK), f32)
    for k in range(4):
        total = jnp.sum(acc[k], axis=1, keepdims=True)
        packed = jnp.where(lane == k, jnp.broadcast_to(total, (BLK, BLK)), packed)
    return -jnp.transpose(packed)[:8]


def ranks(flags, lane):
    rank = flags.astype(i32)
    for shift in (1, 2, 4, 8):
        rank = rank + jnp.where(lane >= shift, pltpu.roll(rank, shift, 1), 0)
    return rank


def nth(flags, rank, n, values):
    return jnp.sum(jnp.where(flags & (rank == n), values, 0), axis=1, keepdims=True)


def exchange_kernel(
    let_in, count_in, part_in, near_in, cell_in, parts_in, cells_in,
    acc, t_ref, pool0, pool1, pool2, left_lists,
    let_list, let_count, part_list, near_lists, cell_lists, cell_ids,
    cells, parts, own_cells, own_rows, chosen0, chosen1, chosen2, npick, npool,
    ids_v, count_v, list_v, list0, list1,
    send_sem, recv_sem, send_n, recv_n, local_sem,
):
    gx = lax.axis_index("gx")
    gy = lax.axis_index("gy")
    me = gx * 8 + gy
    cx, cz = gx // 4, lax.rem(gx, 4)
    cy, cc = gy // 2, lax.rem(gy, 2)
    px = [lax.rem(cx + m, 4) * 4 for m in range(4)]
    py = [lax.rem(cy + m, 4) * 2 for m in range(4)]

    def to_all(action):
        def batch(h, carry, skip=False):
            pz = [lax.rem(cz + h + m, 4) for m in range(4)]
            core = lax.rem(cc + h // 4, 2)
            for b in range(4):
                for a in range(4):
                    if skip and a == 0 and b == 0:
                        continue
                    dy = (a + b) % 4
                    action(px[a] + pz[(2 * a + dy) % 4], py[dy] + core)
            return carry

        batch(0, 0, True)
        lax.fori_loop(1, 8, batch, 0)

    barrier = pltpu.get_barrier_semaphore()

    def greet(ngx, ngy):
        pl.semaphore_signal(barrier, inc=1, device_id=(ngx, ngy), device_id_type=MESH)

    loads = [
        pltpu.make_async_copy(source, target, local_sem.at[n])
        for n, (source, target) in enumerate(
            (
                (cells_in, cells),
                (parts_in, parts),
                (let_in, let_list),
                (count_in, let_count),
                (part_in, part_list),
                (near_in, near_lists),
                (cell_in, cell_lists),
                (cell_in, cell_ids),
            )
        )
    ]
    for load in loads:
        load.start()
    to_all(greet)
    for load in loads:
        load.wait()

    order = (0, 1, 2, 3, 4, 5, 7, 8, 9)

    def own_block(b, carry):
        at = pl.ds(pl.multiple_of(b * BLK, BLK), BLK)
        for r, source in enumerate(order):
            own_cells[b * ROWS + r] = cells[source : source + 1, at]
        return carry

    lax.fori_loop(0, NCB, own_block, 0, unroll=8)

    def own_parts(b, carry):
        at = pl.ds(pl.multiple_of(b * BLK, BLK), BLK)
        for r in range(4):
            own_rows[b * 4 + r] = parts[r : r + 1, at]
        return carry

    lax.fori_loop(0, NBLK, own_parts, 0, unroll=8)

    for position, offset in enumerate(near_offsets):
        target = me + offset
        keep = jnp.where((target >= 0) & (target < DEV), 1.0, 0.0).astype(f32)
        for b in range(4):
            first = part_list[position, b] * 4
            for r in range(4):
                npick[position * 16 + b * 4 + r] = own_rows[first + r] * keep

    def choose0(d, carry):
        first = let_list[0, d] * ROWS
        for r in range(ROWS):
            chosen0[d * ROWS + r] = own_cells[first + r]
        return carry

    lax.fori_loop(0, DEV, choose0, 0, unroll=8)

    def choose_others(d, carry):
        count = let_count[0, d]
        for k, (chosen, base) in enumerate(
            ((chosen1, d * ONE), (chosen2, d * LATE), (chosen2, d * LATE + ROWS)), 1
        ):
            live = jnp.where(k < count, 1.0, 0.0).astype(f32)
            first = let_list[k, d] * ROWS
            for r in range(ROWS):
                chosen[base + r] = own_cells[first + r] * live
        chosen1[d * ONE + ROWS] = jnp.full((1, BLK), count.astype(f32))
        return carry

    lax.fori_loop(0, DEV, choose_others, 0, unroll=4)

    pl.semaphore_wait(barrier, DEV - 1)

    for position, offset in enumerate(near_offsets):
        d = lax.rem(me + offset + DEV, DEV)
        pltpu.make_async_remote_copy(
            npick.at[pl.ds(position * 16, 16)],
            npool.at[pl.ds(NBLK * 4 + position * 16, 16)],
            send_n.at[position],
            recv_n.at[position],
            device_id=(d // 8, lax.rem(d, 8)),
            device_id_type=MESH,
        ).start()

    phases = ((chosen0, pool0, OWN, ROWS), (chosen1, pool1, 0, ONE), (chosen2, pool2, 0, LATE))

    def send_all(phase):
        chosen, pool, base, rows = phases[phase]

        def send(ngx, ngy):
            pltpu.make_async_remote_copy(
                chosen.at[pl.ds((ngx * 8 + ngy) * rows, rows)],
                pool.at[pl.ds(base + me * rows, rows)],
                send_sem.at[phase],
                recv_sem.at[phase],
                device_id=(ngx, ngy),
                device_id_type=MESH,
            ).start()

        to_all(send)

    def wait_all(phase):
        chosen, pool, base, rows = phases[phase]
        pltpu.make_async_remote_copy(
            chosen.at[pl.ds(0, (DEV - 1) * rows)],
            pool.at[pl.ds(base, (DEV - 1) * rows)],
            send_sem.at[phase],
            recv_sem.at[phase],
            device_id=(gx, gy),
            device_id_type=MESH,
        ).wait()

    send_all(0)

    for r in range(ROWS):
        pool0[ZERO + r] = jnp.zeros((1, BLK), f32)

    lane = lax.broadcasted_iota(i32, (NBLK, BLK), 1)
    ids_v[...] = jnp.full((NBLK, BLK), -1, i32)
    ids_v[:, :LC] = cell_ids[...]
    ids = ids_v[...]
    remote = jnp.maximum(ids - NCB, 0)
    slot = remote & 3
    sender = remote >> 2
    listed = ids >= 0
    own = listed & (ids < NCB)
    far = ids >= NCB
    in0 = own | (far & (slot == 0))
    row0 = jnp.where(own, ids * ROWS, OWN + sender * ROWS)
    rank0 = ranks(in0, lane)
    packed = jnp.full((NBLK, BLK), ZERO, i32)
    for p in range(N0):
        packed = jnp.where(lane == p, ZERO - nth(in0, rank0, p + 1, ZERO - row0), packed)
    list_v[...] = packed
    to_list0 = pltpu.make_async_copy(list_v, list0, local_sem.at[7])
    to_list0.start()

    own_copies = [
        pltpu.make_async_copy(own_cells, pool0.at[pl.ds(0, OWN)], local_sem.at[0]),
        pltpu.make_async_copy(own_rows, npool.at[pl.ds(0, NBLK * 4)], local_sem.at[1]),
    ] + [
        pltpu.make_async_copy(
            chosen.at[pl.ds(me * rows, rows)],
            pool.at[pl.ds(base + me * rows, rows)],
            local_sem.at[2 + phase],
        )
        for phase, (chosen, pool, base, rows) in enumerate(phases)
    ]
    for copy in own_copies:
        copy.start()

    send_all(1)

    def spread(j, carry):
        at = pl.ds(pl.multiple_of(j * BLK, BLK), BLK)
        cols = jnp.transpose(parts[:, at])
        for c in range(3):
            t_ref[j * 3 + c] = jnp.broadcast_to(cols[:, c : c + 1], (BLK, BLK))
        return carry

    lax.fori_loop(0, NBLK, spread, 0, unroll=4)

    to_list0.wait()
    for copy in own_copies:
        copy.wait()
    for position in range(4):
        pltpu.make_async_remote_copy(
            npick.at[pl.ds(position * 16, 16)],
            npool.at[pl.ds(NBLK * 4 + position * 16, 16)],
            send_n.at[position],
            recv_n.at[position],
            device_id=(gx, gy),
            device_id_type=MESH,
        ).wait()

    def near_block(j, carry):
        acc[j] = jnp.zeros((4, BLK, BLK), f32)

        def item(i, inner):
            near_item(t_ref, j * 3, npool, [near_lists[i * 2 + k, j] for k in range(2)], acc.at[j])
            return inner

        lax.fori_loop(0, LP // 2, item, 0)
        return carry

    lax.fori_loop(0, NEAR_FIRST, near_block, 0)
    send_all(2)
    lax.fori_loop(NEAR_FIRST, NBLK, near_block, 0)

    wait_all(0)

    def block0(j, carry):
        cell_items(
            N0, lambda i: rows_of(pool0, list0[j, i], ROWS), t_ref, j * 3, acc.at[j]
        )
        return carry

    lax.fori_loop(0, NBLK, block0, 0)

    wait_all(1)

    row_lane = lax.broadcasted_iota(i32, (1, BLK), 1)

    def gather_counts(j, carry):
        counts = jnp.zeros((1, BLK), f32)
        for i in range(LC):
            sender_i = jnp.maximum(cell_lists[j, i] - NCB, 0) >> 2
            counts = jnp.where(row_lane == i, pool1[sender_i * ONE + ROWS], counts)
        count_v[j] = counts
        return carry

    lax.fori_loop(0, NBLK, gather_counts, 0, unroll=2)
    counts = count_v[...].reshape(NBLK, BLK)
    live = slot.astype(f32) < counts
    in1 = (in0 & (rank0 > N0)) | (far & (slot == 1) & live)
    in2 = far & (slot >= 2) & live
    row1 = jnp.where(in0, row0, ROWS0 + sender * ONE)
    row2 = sender * LATE + (slot - 2) * ROWS
    rank1 = ranks(in1, lane)
    rank2 = ranks(in2, lane)
    packed = jnp.full((NBLK, BLK), ZERO, i32)
    for p in range(N1):
        packed = jnp.where(lane == p, ZERO - nth(in1, rank1, p + 1, ZERO - row1), packed)
    list_v[...] = packed
    to_list1 = pltpu.make_async_copy(list_v, list1, local_sem.at[0])
    to_list1.start()
    n1 = jnp.sum(in1.astype(i32), axis=1, keepdims=True)
    n2 = jnp.sum(in2.astype(i32), axis=1, keepdims=True)
    packed = jnp.where(lane == 2 * LC, jnp.maximum(n1 - N1, 0), n2)
    for p in range(LC - N1):
        packed = jnp.where(lane == p, nth(in1, rank1, N1 + p + 1, row1), packed)
    for p in range(LC):
        packed = jnp.where(lane == LC + p, nth(in2, rank2, p + 1, row2), packed)
    left_lists[...] = packed
    to_list1.wait()

    def block1(j, carry):
        cell_items(
            N1, lambda i: rows_of_two(pool0, pool1, list1[j, i]), t_ref, j * 3, acc.at[j]
        )
        return carry

    lax.fori_loop(0, NBLK, block1, 0)

    wait_all(2)


def rest_kernel(lists, acc_in, t_ref, pool0, pool1, pool2, out, acc):
    def block(j, carry):
        cell_items(
            lists[j, 2 * LC],
            lambda i: rows_of_two(pool0, pool1, lists[j, i]),
            t_ref, j * 3, acc.at[j],
        )
        cell_items(
            lists[j, 2 * LC + 1],
            lambda i: rows_of(pool2, lists[j, LC + i], ROWS),
            t_ref, j * 3, acc.at[j],
        )
        return carry

    lax.fori_loop(0, NBLK, block, 0)

    def finish(j, carry):
        out[:, pl.ds(pl.multiple_of(j * BLK, BLK), BLK)] = lane_totals(acc.at[j])[:4]
        return carry

    lax.fori_loop(0, NBLK, finish, 0, unroll=4)


def body(particles, tree_cells, let_list, let_count, part_list, cell_lists, near_lists):
    smem = pl.BlockSpec(memory_space=pltpu.SMEM)
    vmem = pl.BlockSpec(memory_space=pltpu.VMEM)
    hbm = pl.BlockSpec(memory_space=pltpu.HBM)

    def rows(count):
        return pltpu.VMEM((count, 1, BLK), f32)

    acc_shape = (NBLK, 4, BLK, BLK)
    outs = pl.pallas_call(
        exchange_kernel,
        out_shape=(
            pltpu.VMEM(acc_shape, f32),
            pltpu.VMEM((3 * NBLK, BLK, BLK), f32),
            rows(ROWS0),
            rows(ROWS1),
            rows(ROWS2),
            pltpu.VMEM((NBLK, BLK), i32),
        ),
        in_specs=[hbm] * 7,
        out_specs=(vmem,) * 6,
        scratch_shapes=[
            pltpu.SMEM((4, DEV), i32),
            pltpu.SMEM((1, DEV), i32),
            pltpu.SMEM((4, 4), i32),
            pltpu.SMEM((LP, NBLK), i32),
            pltpu.SMEM((NBLK, LC), i32),
            pltpu.VMEM((NBLK, LC), i32),
            pltpu.VMEM(tree_cells.shape, f32),
            pltpu.VMEM(particles.shape, f32),
            rows(OWN),
            rows(NBLK * 4),
            rows(DEV * ROWS),
            rows(DEV * ONE),
            rows(DEV * LATE),
            rows(4 * 16),
            rows(2 * NBLK * 4),
            pltpu.VMEM((NBLK, BLK), i32),
            pltpu.VMEM((NBLK, 1, BLK), f32),
            pltpu.VMEM((NBLK, BLK), i32),
            pltpu.SMEM((NBLK, BLK), i32),
            pltpu.SMEM((NBLK, BLK), i32),
            pltpu.SemaphoreType.DMA((3,)),
            pltpu.SemaphoreType.DMA((3,)),
            pltpu.SemaphoreType.DMA((4,)),
            pltpu.SemaphoreType.DMA((4,)),
            pltpu.SemaphoreType.DMA((8,)),
        ],
        compiler_params=pltpu.CompilerParams(
            collective_id=0, has_side_effects=True, vmem_limit_bytes=24 << 20
        ),
        name="exchange",
    )(
        *[pltpu.with_memory_space_constraint(q, pltpu.HBM) for q in (jnp.transpose(let_list[0]), let_count, part_list[0],
        jnp.transpose(near_lists), cell_lists)], pltpu.with_memory_space_constraint(particles, pltpu.HBM), pltpu.with_memory_space_constraint(tree_cells, pltpu.HBM),
    )
    return pl.pallas_call(
        rest_kernel,
        out_shape=(jax.ShapeDtypeStruct(particles.shape, f32), pltpu.VMEM(acc_shape, f32)),
        in_specs=[smem] + [vmem] * 5,
        out_specs=(vmem, vmem),
        input_output_aliases={1: 1},
        compiler_params=pltpu.CompilerParams(vmem_limit_bytes=24 << 20),
        name="rest",
    )(outs[5], *outs[:5])[0]


def solution(mesh):
    return jax.shard_map(
        body,
        mesh=mesh,
        in_specs=(
            P(None, ("gx", "gy")),
            P(None, ("gx", "gy")),
            P(("gx", "gy"), None, None),
            P(("gx", "gy"), None),
            P(("gx", "gy"), None, None),
            P(("gx", "gy"), None),
            P(("gx", "gy"), None),
        ),
        out_specs=P(None, ("gx", "gy")),
        check_vma=False,
    )
```

```python
import jax
import jax.numpy as jnp
from jax import lax
from jax.experimental import pallas as pl
from jax.experimental.pallas import tpu as pltpu
from jax.sharding import PartitionSpec as P

BLK = 128
NBLK = 16
NCB = 64
DEV = 128
LC = 16
LP = 8
ROWS = 9
EPS = 0.0025
MESH = pl.DeviceIdType.MESH
near_offsets = (1, -1, 2, -2)

OWN = NCB * ROWS
ZERO = OWN + DEV * ROWS
ROWS0 = ZERO + ROWS
ONE = ROWS + 1
ROWS1 = DEV * ONE
LATE = 2 * ROWS
ROWS2 = DEV * LATE
N0 = 4
N1 = 4
NEAR_FIRST = 4

f32 = jnp.float32
i32 = jnp.int32


def rows_of(ref, first, count):
    return [jnp.broadcast_to(ref[first + r], (8, BLK)) for r in range(count)]


def rows_of_two(pool0, pool1, entry):
    other = entry >= ROWS0
    first0 = jnp.where(other, 0, entry)
    first1 = jnp.where(other, entry - ROWS0, 0)
    return [
        jnp.broadcast_to(jnp.where(other, pool1[first1 + r], pool0[first0 + r]), (8, BLK))
        for r in range(ROWS)
    ]


def cell_item(t_ref, t_base, sources, acc):
    def tile(t, carry):
        s = pl.ds(pl.multiple_of(t * 8, 8), 8)
        tx, ty, tz = t_ref[t_base, s], t_ref[t_base + 1, s], t_ref[t_base + 2, s]
        sums = [acc[k, s] for k in range(4)]
        for X, Y, Z, M, Qxx, Qyy, Qxy, Qxz, Qyz in sources:
            x = tx - X
            y = ty - Y
            z = tz - Z
            u = lax.rsqrt(x * x + y * y + z * z + EPS)
            u2 = u * u
            u5 = u * u2 * u2
            x5 = u5 * x
            y5 = u5 * y
            z5 = u5 * z
            qx = Qxx * x5 + Qxy * y5 + Qxz * z5
            qy = Qxy * x5 + Qyy * y5 + Qyz * z5
            qz = Qxz * x5 + Qyz * y5 - (Qxx + Qyy) * z5
            w = x * qx + y * qy + z * qz
            mu = M * u
            p = u2 * (mu + 2.5 * w)
            for k, term in enumerate((p * x - qx, p * y - qy, p * z - qz, mu + 0.5 * w)):
                sums[k] = sums[k] + term
        for k in range(4):
            acc[k, s] = sums[k]
        return carry

    lax.fori_loop(0, 16, tile, 0, unroll=True)


def cell_items(count, rows_at, t_ref, t_base, acc):
    def pair(i, carry):
        cell_item(t_ref, t_base, [rows_at(2 * i), rows_at(2 * i + 1)], acc)
        return carry

    def single(i, carry):
        cell_item(t_ref, t_base, [rows_at(i)], acc)
        return carry

    pairs = count // 2 if isinstance(count, int) else count >> 1
    lax.fori_loop(0, pairs, pair, 0)
    if not isinstance(count, int) or count % 2:
        lax.fori_loop(2 * pairs, count, single, 0)


def near_item(t_ref, t_base, pool, blocks, acc):
    sources = [rows_of(pool, block * 4, 4) for block in blocks]

    def tile(t, carry):
        s = pl.ds(pl.multiple_of(t * 8, 8), 8)
        tx, ty, tz = t_ref[t_base, s], t_ref[t_base + 1, s], t_ref[t_base + 2, s]
        sums = [acc[k, s] for k in range(4)]
        for X, Y, Z, M in sources:
            x = tx - X
            y = ty - Y
            z = tz - Z
            u = lax.rsqrt(x * x + y * y + z * z + EPS)
            mu = M * u
            p = mu * (u * u)
            for k, term in enumerate((p * x, p * y, p * z, mu)):
                sums[k] = sums[k] + term
        for k in range(4):
            acc[k, s] = sums[k]
        return carry

    lax.fori_loop(0, 16, tile, 0, unroll=True)


def lane_totals(acc):
    lane = lax.broadcasted_iota(i32, (BLK, BLK), 1)
    packed = jnp.zeros((BLK, BLK), f32)
    for k in range(4):
        total = jnp.sum(acc[k], axis=1, keepdims=True)
        packed = jnp.where(lane == k, jnp.broadcast_to(total, (BLK, BLK)), packed)
    return -jnp.transpose(packed)[:8]


def ranks(flags, lane):
    rank = flags.astype(i32)
    for shift in (1, 2, 4, 8):
        rank = rank + jnp.where(lane >= shift, pltpu.roll(rank, shift, 1), 0)
    return rank


def nth(flags, rank, n, values):
    return jnp.sum(jnp.where(flags & (rank == n), values, 0), axis=1, keepdims=True)


def exchange_kernel(
    let_in, count_in, part_in, near_in, cell_in, parts_in, cells_in,
    acc, t_ref, pool0, pool1, pool2, left_lists,
    let_list, let_count, part_list, near_lists, cell_lists, cell_ids,
    cells, parts, own_cells, own_rows, chosen0, chosen1, chosen2, npick, npool,
    ids_v, count_v, list_v, list0, list1,
    send_sem, recv_sem, send_n, recv_n, local_sem,
):
    gx = lax.axis_index("gx")
    gy = lax.axis_index("gy")
    me = gx * 8 + gy
    cx, cz = gx // 4, lax.rem(gx, 4)
    cy, cc = gy // 2, lax.rem(gy, 2)
    px = [lax.rem(cx + m, 4) * 4 for m in range(4)]
    py = [lax.rem(cy + m, 4) * 2 for m in range(4)]

    def to_all(action):
        def batch(h, carry, skip=False):
            pz = [lax.rem(cz + h + m, 4) for m in range(4)]
            core = lax.rem(cc + h // 4, 2)
            for b in range(4):
                for a in range(4):
                    if skip and a == 0 and b == 0:
                        continue
                    dy = (a + b) % 4
                    action(px[a] + pz[(2 * a + dy) % 4], py[dy] + core)
            return carry

        batch(0, 0, True)
        lax.fori_loop(1, 8, batch, 0)

    barrier = pltpu.get_barrier_semaphore()

    pz_all = [lax.rem(cz + m, 4) for m in range(4)]
    cores = [cc, 1 - cc]
    hops = (0, 1, 2, 1)
    steps = [
        (hops[dx] + hops[dy] + hops[dz], dx, dy, dz, dc)
        for dx in range(4)
        for dy in range(4)
        for dz in range(4)
        for dc in range(2)
    ]

    def greet_all():
        for far, dx, dy, dz, dc in sorted(steps, reverse=True)[:-1]:
            pl.semaphore_signal(
                barrier,
                inc=1,
                device_id=(px[dx] + pz_all[dz], py[dy] + cores[dc]),
                device_id_type=MESH,
            )

    loads = [
        pltpu.make_async_copy(source, target, local_sem.at[n])
        for n, (source, target) in enumerate(
            (
                (cells_in, cells),
                (parts_in, parts),
                (let_in, let_list),
                (count_in, let_count),
                (part_in, part_list),
                (near_in, near_lists),
                (cell_in, cell_lists),
                (cell_in, cell_ids),
            )
        )
    ]
    for load in loads:
        load.start()
    greet_all()
    for load in loads:
        load.wait()

    order = (0, 1, 2, 3, 4, 5, 7, 8, 9)

    def own_block(b, carry):
        at = pl.ds(pl.multiple_of(b * BLK, BLK), BLK)
        for r, source in enumerate(order):
            own_cells[b * ROWS + r] = cells[source : source + 1, at]
        return carry

    lax.fori_loop(0, NCB, own_block, 0, unroll=8)

    def own_parts(b, carry):
        at = pl.ds(pl.multiple_of(b * BLK, BLK), BLK)
        for r in range(4):
            own_rows[b * 4 + r] = parts[r : r + 1, at]
        return carry

    lax.fori_loop(0, NBLK, own_parts, 0, unroll=8)

    for position, offset in enumerate(near_offsets):
        target = me + offset
        keep = jnp.where((target >= 0) & (target < DEV), 1.0, 0.0).astype(f32)
        for b in range(4):
            first = part_list[position, b] * 4
            for r in range(4):
                npick[position * 16 + b * 4 + r] = own_rows[first + r] * keep

    def choose0(d, carry):
        first = let_list[0, d] * ROWS
        for r in range(ROWS):
            chosen0[d * ROWS + r] = own_cells[first + r]
        return carry

    lax.fori_loop(0, DEV, choose0, 0, unroll=8)

    def choose_others(d, carry):
        count = let_count[0, d]
        for k, (chosen, base) in enumerate(
            ((chosen1, d * ONE), (chosen2, d * LATE), (chosen2, d * LATE + ROWS)), 1
        ):
            live = jnp.where(k < count, 1.0, 0.0).astype(f32)
            first = let_list[k, d] * ROWS
            for r in range(ROWS):
                chosen[base + r] = own_cells[first + r] * live
        chosen1[d * ONE + ROWS] = jnp.full((1, BLK), count.astype(f32))
        return carry

    lax.fori_loop(0, DEV, choose_others, 0, unroll=4)

    pl.semaphore_wait(barrier, DEV - 1)

    for position, offset in enumerate(near_offsets):
        d = lax.rem(me + offset + DEV, DEV)
        pltpu.make_async_remote_copy(
            npick.at[pl.ds(position * 16, 16)],
            npool.at[pl.ds(NBLK * 4 + position * 16, 16)],
            send_n.at[position],
            recv_n.at[position],
            device_id=(d // 8, lax.rem(d, 8)),
            device_id_type=MESH,
        ).start()

    phases = ((chosen0, pool0, OWN, ROWS), (chosen1, pool1, 0, ONE), (chosen2, pool2, 0, LATE))

    def send_all(phase):
        chosen, pool, base, rows = phases[phase]

        def send(ngx, ngy):
            pltpu.make_async_remote_copy(
                chosen.at[pl.ds((ngx * 8 + ngy) * rows, rows)],
                pool.at[pl.ds(base + me * rows, rows)],
                send_sem.at[phase],
                recv_sem.at[phase],
                device_id=(ngx, ngy),
                device_id_type=MESH,
            ).start()

        to_all(send)

    def wait_all(phase):
        chosen, pool, base, rows = phases[phase]
        pltpu.make_async_remote_copy(
            chosen.at[pl.ds(0, (DEV - 1) * rows)],
            pool.at[pl.ds(base, (DEV - 1) * rows)],
            send_sem.at[phase],
            recv_sem.at[phase],
            device_id=(gx, gy),
            device_id_type=MESH,
        ).wait()

    send_all(0)

    for r in range(ROWS):
        pool0[ZERO + r] = jnp.zeros((1, BLK), f32)

    lane = lax.broadcasted_iota(i32, (NBLK, BLK), 1)
    ids_v[...] = jnp.full((NBLK, BLK), -1, i32)
    ids_v[:, :LC] = cell_ids[...]
    ids = ids_v[...]
    remote = jnp.maximum(ids - NCB, 0)
    slot = remote & 3
    sender = remote >> 2
    listed = ids >= 0
    own = listed & (ids < NCB)
    far = ids >= NCB
    in0 = own | (far & (slot == 0))
    row0 = jnp.where(own, ids * ROWS, OWN + sender * ROWS)
    rank0 = ranks(in0, lane)
    packed = jnp.full((NBLK, BLK), ZERO, i32)
    for p in range(N0):
        packed = jnp.where(lane == p, ZERO - nth(in0, rank0, p + 1, ZERO - row0), packed)
    list_v[...] = packed
    to_list0 = pltpu.make_async_copy(list_v, list0, local_sem.at[7])
    to_list0.start()

    own_copies = [
        pltpu.make_async_copy(own_cells, pool0.at[pl.ds(0, OWN)], local_sem.at[0]),
        pltpu.make_async_copy(own_rows, npool.at[pl.ds(0, NBLK * 4)], local_sem.at[1]),
    ] + [
        pltpu.make_async_copy(
            chosen.at[pl.ds(me * rows, rows)],
            pool.at[pl.ds(base + me * rows, rows)],
            local_sem.at[2 + phase],
        )
        for phase, (chosen, pool, base, rows) in enumerate(phases)
    ]
    for copy in own_copies:
        copy.start()

    send_all(1)

    def spread(j, carry):
        at = pl.ds(pl.multiple_of(j * BLK, BLK), BLK)
        cols = jnp.transpose(parts[:, at])
        for c in range(3):
            t_ref[j * 3 + c] = jnp.broadcast_to(cols[:, c : c + 1], (BLK, BLK))
        return carry

    lax.fori_loop(0, NBLK, spread, 0, unroll=4)

    to_list0.wait()
    for copy in own_copies:
        copy.wait()
    for position in range(4):
        pltpu.make_async_remote_copy(
            npick.at[pl.ds(position * 16, 16)],
            npool.at[pl.ds(NBLK * 4 + position * 16, 16)],
            send_n.at[position],
            recv_n.at[position],
            device_id=(gx, gy),
            device_id_type=MESH,
        ).wait()

    def near_block(j, carry):
        acc[j] = jnp.zeros((4, BLK, BLK), f32)

        def item(i, inner):
            near_item(t_ref, j * 3, npool, [near_lists[i * 2 + k, j] for k in range(2)], acc.at[j])
            return inner

        lax.fori_loop(0, LP // 2, item, 0)
        return carry

    lax.fori_loop(0, NEAR_FIRST, near_block, 0)
    send_all(2)
    lax.fori_loop(NEAR_FIRST, NBLK, near_block, 0)

    wait_all(0)

    def block0(j, carry):
        cell_items(
            N0, lambda i: rows_of(pool0, list0[j, i], ROWS), t_ref, j * 3, acc.at[j]
        )
        return carry

    lax.fori_loop(0, NBLK, block0, 0)

    wait_all(1)

    row_lane = lax.broadcasted_iota(i32, (1, BLK), 1)

    def gather_counts(j, carry):
        counts = jnp.zeros((1, BLK), f32)
        for i in range(LC):
            sender_i = jnp.maximum(cell_lists[j, i] - NCB, 0) >> 2
            counts = jnp.where(row_lane == i, pool1[sender_i * ONE + ROWS], counts)
        count_v[j] = counts
        return carry

    lax.fori_loop(0, NBLK, gather_counts, 0, unroll=2)
    counts = count_v[...].reshape(NBLK, BLK)
    live = slot.astype(f32) < counts
    in1 = (in0 & (rank0 > N0)) | (far & (slot == 1) & live)
    in2 = far & (slot >= 2) & live
    row1 = jnp.where(in0, row0, ROWS0 + sender * ONE)
    row2 = sender * LATE + (slot - 2) * ROWS
    rank1 = ranks(in1, lane)
    rank2 = ranks(in2, lane)
    packed = jnp.full((NBLK, BLK), ZERO, i32)
    for p in range(N1):
        packed = jnp.where(lane == p, ZERO - nth(in1, rank1, p + 1, ZERO - row1), packed)
    list_v[...] = packed
    to_list1 = pltpu.make_async_copy(list_v, list1, local_sem.at[0])
    to_list1.start()
    n1 = jnp.sum(in1.astype(i32), axis=1, keepdims=True)
    n2 = jnp.sum(in2.astype(i32), axis=1, keepdims=True)
    packed = jnp.where(lane == 2 * LC, jnp.maximum(n1 - N1, 0), n2)
    for p in range(LC - N1):
        packed = jnp.where(lane == p, nth(in1, rank1, N1 + p + 1, row1), packed)
    for p in range(LC):
        packed = jnp.where(lane == LC + p, nth(in2, rank2, p + 1, row2), packed)
    left_lists[...] = packed
    to_list1.wait()

    def block1(j, carry):
        cell_items(
            N1, lambda i: rows_of_two(pool0, pool1, list1[j, i]), t_ref, j * 3, acc.at[j]
        )
        return carry

    lax.fori_loop(0, NBLK, block1, 0)

    wait_all(2)


def rest_kernel(lists, acc_in, t_ref, pool0, pool1, pool2, out, acc):
    def block(j, carry):
        cell_items(
            lists[j, 2 * LC],
            lambda i: rows_of_two(pool0, pool1, lists[j, i]),
            t_ref, j * 3, acc.at[j],
        )
        cell_items(
            lists[j, 2 * LC + 1],
            lambda i: rows_of(pool2, lists[j, LC + i], ROWS),
            t_ref, j * 3, acc.at[j],
        )
        return carry

    lax.fori_loop(0, NBLK, block, 0)

    def finish(j, carry):
        out[:, pl.ds(pl.multiple_of(j * BLK, BLK), BLK)] = lane_totals(acc.at[j])[:4]
        return carry

    lax.fori_loop(0, NBLK, finish, 0, unroll=8)


def body(particles, tree_cells, let_list, let_count, part_list, cell_lists, near_lists):
    smem = pl.BlockSpec(memory_space=pltpu.SMEM)
    vmem = pl.BlockSpec(memory_space=pltpu.VMEM)
    hbm = pl.BlockSpec(memory_space=pltpu.HBM)

    def rows(count):
        return pltpu.VMEM((count, 1, BLK), f32)

    acc_shape = (NBLK, 4, BLK, BLK)
    outs = pl.pallas_call(
        exchange_kernel,
        out_shape=(
            pltpu.VMEM(acc_shape, f32),
            pltpu.VMEM((3 * NBLK, BLK, BLK), f32),
            rows(ROWS0),
            rows(ROWS1),
            rows(ROWS2),
            pltpu.VMEM((NBLK, BLK), i32),
        ),
        in_specs=[hbm] * 7,
        out_specs=(vmem,) * 6,
        scratch_shapes=[
            pltpu.SMEM((4, DEV), i32),
            pltpu.SMEM((1, DEV), i32),
            pltpu.SMEM((4, 4), i32),
            pltpu.SMEM((LP, NBLK), i32),
            pltpu.SMEM((NBLK, LC), i32),
            pltpu.VMEM((NBLK, LC), i32),
            pltpu.VMEM(tree_cells.shape, f32),
            pltpu.VMEM(particles.shape, f32),
            rows(OWN),
            rows(NBLK * 4),
            rows(DEV * ROWS),
            rows(DEV * ONE),
            rows(DEV * LATE),
            rows(4 * 16),
            rows(2 * NBLK * 4),
            pltpu.VMEM((NBLK, BLK), i32),
            pltpu.VMEM((NBLK, 1, BLK), f32),
            pltpu.VMEM((NBLK, BLK), i32),
            pltpu.SMEM((NBLK, BLK), i32),
            pltpu.SMEM((NBLK, BLK), i32),
            pltpu.SemaphoreType.DMA((3,)),
            pltpu.SemaphoreType.DMA((3,)),
            pltpu.SemaphoreType.DMA((4,)),
            pltpu.SemaphoreType.DMA((4,)),
            pltpu.SemaphoreType.DMA((8,)),
        ],
        compiler_params=pltpu.CompilerParams(
            collective_id=0, has_side_effects=True, vmem_limit_bytes=24 << 20
        ),
        name="exchange",
    )(
        *[pltpu.with_memory_space_constraint(q, pltpu.HBM) for q in (jnp.transpose(let_list[0]), let_count, part_list[0],
        jnp.transpose(near_lists), cell_lists)], pltpu.with_memory_space_constraint(particles, pltpu.HBM), pltpu.with_memory_space_constraint(tree_cells, pltpu.HBM),
    )
    return pl.pallas_call(
        rest_kernel,
        out_shape=(jax.ShapeDtypeStruct(particles.shape, f32), pltpu.VMEM(acc_shape, f32)),
        in_specs=[smem] + [vmem] * 5,
        out_specs=(vmem, vmem),
        input_output_aliases={1: 1},
        compiler_params=pltpu.CompilerParams(vmem_limit_bytes=24 << 20),
        name="rest",
    )(outs[5], *outs[:5])[0]


def solution(mesh):
    return jax.shard_map(
        body,
        mesh=mesh,
        in_specs=(
            P(None, ("gx", "gy")),
            P(None, ("gx", "gy")),
            P(("gx", "gy"), None, None),
            P(("gx", "gy"), None),
            P(("gx", "gy"), None, None),
            P(("gx", "gy"), None),
            P(("gx", "gy"), None),
        ),
        out_specs=P(None, ("gx", "gy")),
        check_vma=False,
    )
```

```python
import jax
import jax.numpy as jnp
from jax import lax
from jax.experimental import pallas as pl
from jax.experimental.pallas import tpu as pltpu
from jax.sharding import PartitionSpec as P

BLK = 128
NBLK = 16
NCB = 64
DEV = 128
LC = 16
LP = 8
ROWS = 9
EPS = 0.0025
MESH = pl.DeviceIdType.MESH
near_offsets = (1, -1, 2, -2)

OWN = NCB * ROWS
ZERO = OWN + DEV * ROWS
ROWS0 = ZERO + ROWS
ONE = ROWS + 1
ROWS1 = DEV * ONE
LATE = 2 * ROWS
ROWS2 = DEV * LATE
N0 = 4
N1 = 4
NEAR_FIRST = 4

f32 = jnp.float32
i32 = jnp.int32


def rows_of(ref, first, count):
    return [jnp.broadcast_to(ref[first + r], (8, BLK)) for r in range(count)]


def rows_of_two(pool0, pool1, entry):
    other = entry >= ROWS0
    first0 = jnp.where(other, 0, entry)
    first1 = jnp.where(other, entry - ROWS0, 0)
    return [
        jnp.broadcast_to(jnp.where(other, pool1[first1 + r], pool0[first0 + r]), (8, BLK))
        for r in range(ROWS)
    ]


def cell_item(t_ref, t_base, sources, acc):
    def tile(t, carry):
        s = pl.ds(pl.multiple_of(t * 8, 8), 8)
        tx, ty, tz = t_ref[t_base, s], t_ref[t_base + 1, s], t_ref[t_base + 2, s]
        sums = [acc[k, s] for k in range(4)]
        for X, Y, Z, M, Qxx, Qyy, Qxy, Qxz, Qyz in sources:
            x = tx - X
            y = ty - Y
            z = tz - Z
            u = lax.rsqrt(x * x + y * y + z * z + EPS)
            u2 = u * u
            u5 = u * u2 * u2
            x5 = u5 * x
            y5 = u5 * y
            z5 = u5 * z
            qx = Qxx * x5 + Qxy * y5 + Qxz * z5
            qy = Qxy * x5 + Qyy * y5 + Qyz * z5
            qz = Qxz * x5 + Qyz * y5 - (Qxx + Qyy) * z5
            w = x * qx + y * qy + z * qz
            mu = M * u
            p = u2 * (mu + 2.5 * w)
            for k, term in enumerate((p * x - qx, p * y - qy, p * z - qz, mu + 0.5 * w)):
                sums[k] = sums[k] + term
        for k in range(4):
            acc[k, s] = sums[k]
        return carry

    lax.fori_loop(0, 16, tile, 0, unroll=True)


def cell_items(count, rows_at, t_ref, t_base, acc):
    def pair(i, carry):
        cell_item(t_ref, t_base, [rows_at(2 * i), rows_at(2 * i + 1)], acc)
        return carry

    def single(i, carry):
        cell_item(t_ref, t_base, [rows_at(i)], acc)
        return carry

    pairs = count // 2 if isinstance(count, int) else count >> 1
    lax.fori_loop(0, pairs, pair, 0)
    if not isinstance(count, int) or count % 2:
        lax.fori_loop(2 * pairs, count, single, 0)


def near_item(t_ref, t_base, pool, blocks, acc):
    sources = [rows_of(pool, block * 4, 4) for block in blocks]

    def tile(t, carry):
        s = pl.ds(pl.multiple_of(t * 8, 8), 8)
        tx, ty, tz = t_ref[t_base, s], t_ref[t_base + 1, s], t_ref[t_base + 2, s]
        sums = [acc[k, s] for k in range(4)]
        for X, Y, Z, M in sources:
            x = tx - X
            y = ty - Y
            z = tz - Z
            u = lax.rsqrt(x * x + y * y + z * z + EPS)
            mu = M * u
            p = mu * (u * u)
            for k, term in enumerate((p * x, p * y, p * z, mu)):
                sums[k] = sums[k] + term
        for k in range(4):
            acc[k, s] = sums[k]
        return carry

    lax.fori_loop(0, 16, tile, 0, unroll=True)


def lane_totals(acc):
    lane = lax.broadcasted_iota(i32, (BLK, BLK), 1)
    packed = jnp.zeros((BLK, BLK), f32)
    for k in range(4):
        total = jnp.sum(acc[k], axis=1, keepdims=True)
        packed = jnp.where(lane == k, jnp.broadcast_to(total, (BLK, BLK)), packed)
    return -jnp.transpose(packed)[:8]


def ranks(flags, lane):
    rank = flags.astype(i32)
    for shift in (1, 2, 4, 8):
        rank = rank + jnp.where(lane >= shift, pltpu.roll(rank, shift, 1), 0)
    return rank


def nth(flags, rank, n, values):
    return jnp.sum(jnp.where(flags & (rank == n), values, 0), axis=1, keepdims=True)


def exchange_kernel(
    let_in, count_in, part_in, near_in, cell_in, parts_in, cells_in,
    acc, t_ref, pool0, pool1, pool2, left_lists,
    let_list, let_count, part_list, near_lists, cell_lists, cell_ids,
    cells, parts, own_cells, own_rows, chosen0, chosen1, chosen2, npick, npool,
    ids_v, count_v, list_v, list0, list1,
    send_sem, recv_sem, send_n, recv_n, local_sem,
):
    gx = lax.axis_index("gx")
    gy = lax.axis_index("gy")
    me = gx * 8 + gy
    cx, cz = gx // 4, lax.rem(gx, 4)
    cy, cc = gy // 2, lax.rem(gy, 2)
    px = [lax.rem(cx + m, 4) * 4 for m in range(4)]
    py = [lax.rem(cy + m, 4) * 2 for m in range(4)]

    def to_all(action):
        def batch(h, carry, skip=False):
            pz = [lax.rem(cz + h + m, 4) for m in range(4)]
            core = lax.rem(cc + h // 4, 2)
            for b in range(4):
                for a in range(4):
                    if skip and a == 0 and b == 0:
                        continue
                    dy = (a + b) % 4
                    action(px[a] + pz[(2 * a + dy) % 4], py[dy] + core)
            return carry

        batch(0, 0, True)
        lax.fori_loop(1, 8, batch, 0, unroll=7)

    barrier = pltpu.get_barrier_semaphore()

    pz_all = [lax.rem(cz + m, 4) for m in range(4)]
    cores = [cc, 1 - cc]
    hops = (0, 1, 2, 1)
    steps = [
        (hops[dx] + hops[dy] + hops[dz], dx, dy, dz, dc)
        for dx in range(4)
        for dy in range(4)
        for dz in range(4)
        for dc in range(2)
    ]

    def greet_all():
        for far, dx, dy, dz, dc in sorted(steps, reverse=True)[:-1]:
            pl.semaphore_signal(
                barrier,
                inc=1,
                device_id=(px[dx] + pz_all[dz], py[dy] + cores[dc]),
                device_id_type=MESH,
            )

    loads = [
        pltpu.make_async_copy(source, target, local_sem.at[n])
        for n, (source, target) in enumerate(
            (
                (cells_in, cells),
                (parts_in, parts),
                (let_in, let_list),
                (count_in, let_count),
                (part_in, part_list),
                (near_in, near_lists),
                (cell_in, cell_lists),
                (cell_in, cell_ids),
            )
        )
    ]
    for load in loads:
        load.start()
    greet_all()
    for load in loads:
        load.wait()

    order = (0, 1, 2, 3, 4, 5, 7, 8, 9)

    def own_block(b, carry):
        at = pl.ds(pl.multiple_of(b * BLK, BLK), BLK)
        for r, source in enumerate(order):
            own_cells[b * ROWS + r] = cells[source : source + 1, at]
        return carry

    lax.fori_loop(0, NCB, own_block, 0, unroll=8)

    def own_parts(b, carry):
        at = pl.ds(pl.multiple_of(b * BLK, BLK), BLK)
        for r in range(4):
            own_rows[b * 4 + r] = parts[r : r + 1, at]
        return carry

    lax.fori_loop(0, NBLK, own_parts, 0, unroll=8)

    for position, offset in enumerate(near_offsets):
        target = me + offset
        keep = jnp.where((target >= 0) & (target < DEV), 1.0, 0.0).astype(f32)
        for b in range(4):
            first = part_list[position, b] * 4
            for r in range(4):
                npick[position * 16 + b * 4 + r] = own_rows[first + r] * keep

    def choose0(d, carry):
        first = let_list[0, d] * ROWS
        for r in range(ROWS):
            chosen0[d * ROWS + r] = own_cells[first + r]
        return carry

    lax.fori_loop(0, DEV, choose0, 0, unroll=8)

    def choose_others(d, carry):
        count = let_count[0, d]
        for k, (chosen, base) in enumerate(
            ((chosen1, d * ONE), (chosen2, d * LATE), (chosen2, d * LATE + ROWS)), 1
        ):
            live = jnp.where(k < count, 1.0, 0.0).astype(f32)
            first = let_list[k, d] * ROWS
            for r in range(ROWS):
                chosen[base + r] = own_cells[first + r] * live
        chosen1[d * ONE + ROWS] = jnp.full((1, BLK), count.astype(f32))
        return carry

    lax.fori_loop(0, DEV, choose_others, 0, unroll=4)

    pl.semaphore_wait(barrier, DEV - 1)

    for position, offset in enumerate(near_offsets):
        d = lax.rem(me + offset + DEV, DEV)
        pltpu.make_async_remote_copy(
            npick.at[pl.ds(position * 16, 16)],
            npool.at[pl.ds(NBLK * 4 + position * 16, 16)],
            send_n.at[position],
            recv_n.at[position],
            device_id=(d // 8, lax.rem(d, 8)),
            device_id_type=MESH,
        ).start()

    phases = ((chosen0, pool0, OWN, ROWS), (chosen1, pool1, 0, ONE), (chosen2, pool2, 0, LATE))

    def send_all(phase):
        chosen, pool, base, rows = phases[phase]

        def send(ngx, ngy):
            pltpu.make_async_remote_copy(
                chosen.at[pl.ds((ngx * 8 + ngy) * rows, rows)],
                pool.at[pl.ds(base + me * rows, rows)],
                send_sem.at[phase],
                recv_sem.at[phase],
                device_id=(ngx, ngy),
                device_id_type=MESH,
            ).start()

        to_all(send)

    def wait_all(phase):
        chosen, pool, base, rows = phases[phase]
        pltpu.make_async_remote_copy(
            chosen.at[pl.ds(0, (DEV - 1) * rows)],
            pool.at[pl.ds(base, (DEV - 1) * rows)],
            send_sem.at[phase],
            recv_sem.at[phase],
            device_id=(gx, gy),
            device_id_type=MESH,
        ).wait()

    send_all(0)

    for r in range(ROWS):
        pool0[ZERO + r] = jnp.zeros((1, BLK), f32)

    lane = lax.broadcasted_iota(i32, (NBLK, BLK), 1)
    ids_v[...] = jnp.full((NBLK, BLK), -1, i32)
    ids_v[:, :LC] = cell_ids[...]
    ids = ids_v[...]
    remote = jnp.maximum(ids - NCB, 0)
    slot = remote & 3
    sender = remote >> 2
    listed = ids >= 0
    own = listed & (ids < NCB)
    far = ids >= NCB
    in0 = own | (far & (slot == 0))
    row0 = jnp.where(own, ids * ROWS, OWN + sender * ROWS)
    rank0 = ranks(in0, lane)
    packed = jnp.full((NBLK, BLK), ZERO, i32)
    for p in range(N0):
        packed = jnp.where(lane == p, ZERO - nth(in0, rank0, p + 1, ZERO - row0), packed)
    list_v[...] = packed
    to_list0 = pltpu.make_async_copy(list_v, list0, local_sem.at[7])
    to_list0.start()

    own_copies = [
        pltpu.make_async_copy(own_cells, pool0.at[pl.ds(0, OWN)], local_sem.at[0]),
        pltpu.make_async_copy(own_rows, npool.at[pl.ds(0, NBLK * 4)], local_sem.at[1]),
    ] + [
        pltpu.make_async_copy(
            chosen.at[pl.ds(me * rows, rows)],
            pool.at[pl.ds(base + me * rows, rows)],
            local_sem.at[2 + phase],
        )
        for phase, (chosen, pool, base, rows) in enumerate(phases)
    ]
    for copy in own_copies:
        copy.start()

    send_all(1)

    def spread(j, carry):
        at = pl.ds(pl.multiple_of(j * BLK, BLK), BLK)
        cols = jnp.transpose(parts[:, at])
        for c in range(3):
            t_ref[j * 3 + c] = jnp.broadcast_to(cols[:, c : c + 1], (BLK, BLK))
        return carry

    lax.fori_loop(0, NBLK, spread, 0, unroll=4)

    to_list0.wait()
    for copy in own_copies:
        copy.wait()
    for position in range(4):
        pltpu.make_async_remote_copy(
            npick.at[pl.ds(position * 16, 16)],
            npool.at[pl.ds(NBLK * 4 + position * 16, 16)],
            send_n.at[position],
            recv_n.at[position],
            device_id=(gx, gy),
            device_id_type=MESH,
        ).wait()

    def near_block(j, carry):
        acc[j] = jnp.zeros((4, BLK, BLK), f32)

        def item(i, inner):
            near_item(t_ref, j * 3, npool, [near_lists[i * 2 + k, j] for k in range(2)], acc.at[j])
            return inner

        lax.fori_loop(0, LP // 2, item, 0)
        return carry

    lax.fori_loop(0, NEAR_FIRST, near_block, 0)
    send_all(2)
    lax.fori_loop(NEAR_FIRST, NBLK, near_block, 0)

    wait_all(0)

    def block0(j, carry):
        cell_items(
            N0, lambda i: rows_of(pool0, list0[j, i], ROWS), t_ref, j * 3, acc.at[j]
        )
        return carry

    lax.fori_loop(0, NBLK, block0, 0)

    wait_all(1)

    row_lane = lax.broadcasted_iota(i32, (1, BLK), 1)

    def gather_counts(j, carry):
        counts = jnp.zeros((1, BLK), f32)
        for i in range(LC):
            sender_i = jnp.maximum(cell_lists[j, i] - NCB, 0) >> 2
            counts = jnp.where(row_lane == i, pool1[sender_i * ONE + ROWS], counts)
        count_v[j] = counts
        return carry

    lax.fori_loop(0, NBLK, gather_counts, 0, unroll=2)
    counts = count_v[...].reshape(NBLK, BLK)
    live = slot.astype(f32) < counts
    in1 = (in0 & (rank0 > N0)) | (far & (slot == 1) & live)
    in2 = far & (slot >= 2) & live
    row1 = jnp.where(in0, row0, ROWS0 + sender * ONE)
    row2 = sender * LATE + (slot - 2) * ROWS
    rank1 = ranks(in1, lane)
    rank2 = ranks(in2, lane)
    packed = jnp.full((NBLK, BLK), ZERO, i32)
    for p in range(N1):
        packed = jnp.where(lane == p, ZERO - nth(in1, rank1, p + 1, ZERO - row1), packed)
    list_v[...] = packed
    to_list1 = pltpu.make_async_copy(list_v, list1, local_sem.at[0])
    to_list1.start()
    n1 = jnp.sum(in1.astype(i32), axis=1, keepdims=True)
    n2 = jnp.sum(in2.astype(i32), axis=1, keepdims=True)
    packed = jnp.where(lane == 2 * LC, jnp.maximum(n1 - N1, 0), n2)
    for p in range(LC - N1):
        packed = jnp.where(lane == p, nth(in1, rank1, N1 + p + 1, row1), packed)
    for p in range(LC):
        packed = jnp.where(lane == LC + p, nth(in2, rank2, p + 1, row2), packed)
    left_lists[...] = packed
    to_list1.wait()

    def block1(j, carry):
        cell_items(
            N1, lambda i: rows_of_two(pool0, pool1, list1[j, i]), t_ref, j * 3, acc.at[j]
        )
        return carry

    lax.fori_loop(0, NBLK, block1, 0)

    wait_all(2)


def rest_kernel(lists, acc_in, t_ref, pool0, pool1, pool2, out, acc):
    def block(j, carry):
        cell_items(
            lists[j, 2 * LC],
            lambda i: rows_of_two(pool0, pool1, lists[j, i]),
            t_ref, j * 3, acc.at[j],
        )
        cell_items(
            lists[j, 2 * LC + 1],
            lambda i: rows_of(pool2, lists[j, LC + i], ROWS),
            t_ref, j * 3, acc.at[j],
        )
        return carry

    lax.fori_loop(0, NBLK, block, 0)

    def finish(j, carry):
        out[:, pl.ds(pl.multiple_of(j * BLK, BLK), BLK)] = lane_totals(acc.at[j])[:4]
        return carry

    lax.fori_loop(0, NBLK, finish, 0, unroll=8)


def body(particles, tree_cells, let_list, let_count, part_list, cell_lists, near_lists):
    smem = pl.BlockSpec(memory_space=pltpu.SMEM)
    vmem = pl.BlockSpec(memory_space=pltpu.VMEM)
    hbm = pl.BlockSpec(memory_space=pltpu.HBM)

    def rows(count):
        return pltpu.VMEM((count, 1, BLK), f32)

    acc_shape = (NBLK, 4, BLK, BLK)
    outs = pl.pallas_call(
        exchange_kernel,
        out_shape=(
            pltpu.VMEM(acc_shape, f32),
            pltpu.VMEM((3 * NBLK, BLK, BLK), f32),
            rows(ROWS0),
            rows(ROWS1),
            rows(ROWS2),
            pltpu.VMEM((NBLK, BLK), i32),
        ),
        in_specs=[hbm] * 7,
        out_specs=(vmem,) * 6,
        scratch_shapes=[
            pltpu.SMEM((4, DEV), i32),
            pltpu.SMEM((1, DEV), i32),
            pltpu.SMEM((4, 4), i32),
            pltpu.SMEM((LP, NBLK), i32),
            pltpu.SMEM((NBLK, LC), i32),
            pltpu.VMEM((NBLK, LC), i32),
            pltpu.VMEM(tree_cells.shape, f32),
            pltpu.VMEM(particles.shape, f32),
            rows(OWN),
            rows(NBLK * 4),
            rows(DEV * ROWS),
            rows(DEV * ONE),
            rows(DEV * LATE),
            rows(4 * 16),
            rows(2 * NBLK * 4),
            pltpu.VMEM((NBLK, BLK), i32),
            pltpu.VMEM((NBLK, 1, BLK), f32),
            pltpu.VMEM((NBLK, BLK), i32),
            pltpu.SMEM((NBLK, BLK), i32),
            pltpu.SMEM((NBLK, BLK), i32),
            pltpu.SemaphoreType.DMA((3,)),
            pltpu.SemaphoreType.DMA((3,)),
            pltpu.SemaphoreType.DMA((4,)),
            pltpu.SemaphoreType.DMA((4,)),
            pltpu.SemaphoreType.DMA((8,)),
        ],
        compiler_params=pltpu.CompilerParams(
            collective_id=0, has_side_effects=True, vmem_limit_bytes=24 << 20
        ),
        name="exchange",
    )(
        *[pltpu.with_memory_space_constraint(q, pltpu.HBM) for q in (jnp.transpose(let_list[0]), let_count, part_list[0],
        jnp.transpose(near_lists), cell_lists)], pltpu.with_memory_space_constraint(particles, pltpu.HBM), pltpu.with_memory_space_constraint(tree_cells, pltpu.HBM),
    )
    return pl.pallas_call(
        rest_kernel,
        out_shape=(jax.ShapeDtypeStruct(particles.shape, f32), pltpu.VMEM(acc_shape, f32)),
        in_specs=[smem] + [vmem] * 5,
        out_specs=(vmem, vmem),
        input_output_aliases={1: 1},
        compiler_params=pltpu.CompilerParams(vmem_limit_bytes=24 << 20),
        name="rest",
    )(outs[5], *outs[:5])[0]


def solution(mesh):
    return jax.shard_map(
        body,
        mesh=mesh,
        in_specs=(
            P(None, ("gx", "gy")),
            P(None, ("gx", "gy")),
            P(("gx", "gy"), None, None),
            P(("gx", "gy"), None),
            P(("gx", "gy"), None, None),
            P(("gx", "gy"), None),
            P(("gx", "gy"), None),
        ),
        out_specs=P(None, ("gx", "gy")),
        check_vma=False,
    )
```
